32 devices in a mesh: dp: 8 (over z, y), mp: 4 (over x, core).
Axes of the slice: x: 2, y: 2, z: 4, core: 2. Of those that a mesh axis runs over, the one named last changes fastest.
Arguments:
- patches: bfloat16 [16384, 1024], P(('dp', 'mp')), may hold values from -6 to 6
- cotangent: bfloat16 [16384, 1024], P(('dp', 'mp')), may hold values from -6 to 6
- item_group: int32 [16], replicated, may hold values from 0 to 7, as said below
- item_length: int32 [16], replicated, may hold values from 1 to 1024, as said below
- project_in: float32 [1024, 3, 1024], P(None, None, 'mp'), may hold values from -0.25 to 0.25
- project_out: float32 [1024, 1024], P('mp'), may hold values from -0.75 to 0.75
- expand_weight: float32 [1024, 4096], P(None, 'mp'), may hold values from -0.1875 to 0.1875
- shrink_weight: float32 [4096, 1024], P('mp'), may hold values from -0.09375 to 0.09375
- moment_in: float32 [1024, 3, 1024], P(None, None, 'mp'), may hold values from -512 to 512
- moment_out: float32 [1024, 1024], P('mp'), may hold values from -112 to 112
- moment_expand: float32 [1024, 4096], P(None, 'mp'), may hold values from -160 to 160
- moment_shrink: float32 [4096, 1024], P('mp'), may hold values from -320 to 320
- norm_gains: float32 [2, 1024], replicated, may hold values from 0.5 to 1.5
- shift_rows: float32 [4, 1024], replicated, may hold values from -0.625 to 0.625
- head_shift: float32 [2, 1024], P(None, 'mp'), may hold values from -0.625 to 0.625
- expand_shift: float32 [4096], replicated, may hold values from -0.625 to 0.625
- moment_gains: float32 [2, 1024], replicated, may hold values from -384 to 384
- moment_shifts: float32 [4, 1024], replicated, may hold values from -384 to 384
- moment_head: float32 [2, 1024], P(None, 'mp'), may hold values from -512 to 512
- moment_expand_shift: float32 [4096], replicated, may hold values from -160 to 160
Outputs:
- block_out: bfloat16 [16384, 1024], P(('dp', 'mp'))
- patch_grad: bfloat16 [16384, 1024], P(('dp', 'mp'))
- next_in: float32 [1024, 3, 1024], P(None, None, 'mp')
- next_out: float32 [1024, 1024], P('mp')
- next_expand: float32 [1024, 4096], P(None, 'mp')
- next_shrink: float32 [4096, 1024], P('mp')
- copy_in: bfloat16 [1024, 3, 1024], P(None, None, 'mp')
- copy_out: bfloat16 [1024, 1024], P('mp')
- copy_expand: bfloat16 [1024, 4096], P(None, 'mp')
- copy_shrink: bfloat16 [4096, 1024], P('mp')
- next_moment_in: float32 [1024, 3, 1024], P(None, None, 'mp')
- next_moment_out: float32 [1024, 1024], P('mp')
- next_moment_expand: float32 [1024, 4096], P(None, 'mp')
- next_moment_shrink: float32 [4096, 1024], P('mp')
- next_gains: float32 [2, 1024], replicated
- next_shifts: float32 [4, 1024], replicated
- next_head_shift: float32 [2, 1024], P(None, 'mp')
- next_expand_shift: float32 [4096], replicated
- next_moment_gains: float32 [2, 1024], replicated
- next_moment_shifts: float32 [4, 1024], replicated
- next_moment_head: float32 [2, 1024], P(None, 'mp')
- next_moment_expand_shift: float32 [4096], replicated
The draws below stay inside these ranges and needn't reach their ends.
Inputs may be any that keep to these rules, and one draw needn't show every extreme that they name: `item_group`: each of the 8 groups is named by exactly two items. `item_length`: the items of one group have at most 2048 patches together, and in every draw one group holds exactly 2048.
All inputs are finite; a program needn't handle non-finite values.
Results may differ from the reference program's by a relative error of at most 0.02.
The reference program's roundings to bfloat16 on the way count: a program that leaves them out, or rounds other values in their place, can miss the bound.
Values may be sent and summed in bfloat16 or wider, within the bound.
A program may use at most 192 MiB of HBM per device.

```python
from functools import partial
import jax
import jax.numpy as jnp
from jax import lax

D = 1024
HEADS = 16
HD = 64
FF = 4096
ROWS_GRP = 2048
NS_ITERS = 5
ITEMS = 16
TOKENS = 16384
N_DP = 8


def pack_items(key):
    base_key = jax.random.fold_in(key, 1201)
    slot_key, power_key, jitter_key, full_key = jax.random.split(base_key, 4)
    slot_order = jax.random.permutation(slot_key, ITEMS)
    groups = (slot_order // 2).astype(jnp.int32)
    half_rows = ROWS_GRP // 2
    powers = jax.random.randint(power_key, (ITEMS,), 0, 3)
    base_length = jnp.floor_divide(jnp.int32(half_rows), jnp.left_shift(jnp.int32(1), powers.astype(jnp.int32)))
    jitter = jax.random.randint(jitter_key, (ITEMS,), 0, 1 << 20) % (base_length // 4 + 1)
    lengths = base_length - jitter
    full_group = jax.random.randint(full_key, (), 0, N_DP)
    lengths = jnp.where(groups == full_group, half_rows, lengths).astype(jnp.int32)
    return (groups, lengths)


def draw_item_group(key, part):
    return pack_items(key)[0]


def draw_item_length(key, part):
    return pack_items(key)[1]


def block_scale(own_key, extent, pieces, least, high):
    def one(dim, blocks):
        steps = jax.random.uniform(jax.random.fold_in(jax.random.fold_in(own_key, 6), dim), (blocks,), jnp.float32, least / len(pieces), high / len(pieces))
        return jnp.repeat(jnp.exp(steps), extent[dim] // blocks).reshape((-1,) + (1,) * (len(extent) - dim - 1))

    gain = one(*pieces[0])
    for cut in pieces[1:]:
        gain = gain * one(*cut)
    return gain


def gaussian(rng, dims, width, most, cuts=(), kind=jnp.bfloat16):
    level = block_scale(rng, dims, cuts, -0.22, 0.18) if cuts else 1.0
    values = jax.random.normal(rng, dims, jnp.float32) * width * level
    return jnp.minimum(jnp.maximum(values, -most), most).astype(kind)


def setup_inputs(seed: int = 0) -> dict:
    splits = jax.random.split(jax.random.key(seed), 21)
    patches = gaussian(splits[0], (TOKENS, D), 1.0, 6.0, ((0, 32),))
    cotangent = gaussian(splits[1], (TOKENS, D), 1.0, 6.0, ((0, 32),))
    item_group = draw_item_group(jax.random.fold_in(splits[20], 71), 0)
    item_length = draw_item_length(jax.random.fold_in(splits[20], 71), 0)
    project_in = gaussian(splits[4], (D, 3, D), (D // 2) ** -0.5, 0.25, ((2, 4),), jnp.float32)
    project_out = gaussian(splits[5], (D, D), (D // 16) ** -0.5, 0.75, ((0, 4),), jnp.float32)
    expand_weight = gaussian(splits[6], (D, FF), D ** -0.5, 0.1875, ((1, 4),), jnp.float32)
    shrink_weight = gaussian(splits[7], (FF, D), FF ** -0.5, 0.09375, ((0, 4),), jnp.float32)
    moment_in = gaussian(splits[8], (D, 3, D), (0.7 * TOKENS ** 0.5), 512.0, ((2, 4),), jnp.float32)
    moment_out = gaussian(splits[9], (D, D), (0.15 * TOKENS ** 0.5), 112.0, ((0, 4),), jnp.float32)
    moment_expand = gaussian(splits[10], (D, FF), (0.2 * TOKENS ** 0.5), 160.0, ((1, 4),), jnp.float32)
    moment_shrink = gaussian(splits[11], (FF, D), (0.4 * TOKENS ** 0.5), 320.0, ((0, 4),), jnp.float32)
    norm_gains = jnp.clip(1.0 + 0.1 * jax.random.normal(splits[12], (2, D), jnp.float32), 0.5, 1.5)
    shift_rows = gaussian(splits[13], (4, D), 0.1, 0.625, (), jnp.float32)
    head_shift = gaussian(splits[14], (2, D), 0.1, 0.625, ((1, 4),), jnp.float32)
    expand_shift = gaussian(splits[15], (FF,), 0.1, 0.625, (), jnp.float32)
    moment_gains = gaussian(splits[16], (2, D), (0.5 * TOKENS ** 0.5), 384.0, (), jnp.float32)
    moment_shifts = gaussian(splits[17], (4, D), (0.5 * TOKENS ** 0.5), 384.0, (), jnp.float32)
    moment_head = gaussian(splits[18], (2, D), (0.7 * TOKENS ** 0.5), 512.0, ((1, 4),), jnp.float32)
    moment_expand_shift = gaussian(splits[19], (FF,), (0.2 * TOKENS ** 0.5), 160.0, (), jnp.float32)
    return {"patches": patches, "cotangent": cotangent, "item_group": item_group, "item_length": item_length, "project_in": project_in, "project_out": project_out, "expand_weight": expand_weight, "shrink_weight": shrink_weight, "moment_in": moment_in, "moment_out": moment_out, "moment_expand": moment_expand, "moment_shrink": moment_shrink, "norm_gains": norm_gains, "shift_rows": shift_rows, "head_shift": head_shift, "expand_shift": expand_shift, "moment_gains": moment_gains, "moment_shifts": moment_shifts, "moment_head": moment_head, "moment_expand_shift": moment_expand_shift}


@jax.custom_vjp
def low(v):
    return lax.optimization_barrier(v.astype(jnp.bfloat16)).astype(jnp.float32)

@jax.custom_vjp
def low_back(v):
    return v

def low_keep(v):
    return (low(v), None)

def low_pass(kept, grad):
    return (grad,)

def back_keep(v):
    return (v, None)

def back_low(kept, grad):
    return (low(grad),)
low.defvjp(low_keep, low_pass)
low_back.defvjp(back_keep, back_low)
norm_eps = 1e-06
coef_a = 3.4445
coef_b = -4.775
coef_c = 2.0315
muon_decay = 0.95
plain_decay = 0.5
neg_fill = -1e+30
highest = lax.Precision.HIGHEST

def product(left_side, right_side):
    return jnp.dot(left_side, right_side, precision=highest)

def layer_norm(values, scale_row, shift_row):
    row_mean = lax.optimization_barrier(jnp.mean(values, axis=-1, keepdims=True))
    centered = values - row_mean
    spread = lax.optimization_barrier(jnp.mean(centered * centered, axis=-1, keepdims=True))
    return centered * lax.rsqrt(spread + norm_eps) * scale_row + shift_row

def group_segments(item_group, item_length, group_index):
    member = item_group == group_index
    lengths = jnp.where(member, item_length, 0).astype(jnp.int32)
    item_ends = jnp.cumsum(lengths).astype(jnp.int32)
    item_starts = (item_ends - lengths).astype(jnp.int32)
    row_ids = jnp.arange(ROWS_GRP, dtype=jnp.int32)[:, None]
    inside = (row_ids >= item_starts[None, :]) & (row_ids < item_ends[None, :]) & member[None, :]
    labels = jnp.arange(item_group.shape[0], dtype=jnp.int32)[None, :]
    return lax.optimization_barrier(jnp.max(jnp.where(inside, labels, -1), axis=1)).astype(jnp.int32)

def attention(queries, key_rows, value_rows, segment):
    block_rows = min(512, ROWS_GRP)
    block_count = ROWS_GRP // block_rows
    score_scale = HD ** (-0.5)
    key_heads = key_rows.reshape(ROWS_GRP, HEADS, HD)
    value_heads = value_rows.reshape(ROWS_GRP, HEADS, HD)

    def one_block(block_pair):
        q_block, seg_block = block_pair
        scores = jnp.einsum('qhe,khe->hqk', q_block, key_heads, precision=highest) * score_scale
        scores = low_back(scores)
        allowed = seg_block[:, None] == segment[None, :]
        scores = jnp.where(allowed[None], scores, neg_fill)
        weights = low(jax.nn.softmax(scores, axis=-1))
        return jnp.einsum('hqk,khe->qhe', weights, value_heads, precision=highest)
    blocks = lax.map(jax.checkpoint(one_block), (queries.reshape(block_count, block_rows, HEADS, HD), segment.reshape(block_count, block_rows)))
    return blocks.reshape(ROWS_GRP, D)

def group_forward(group_pair, in_low, out_low, expand_low, shrink_low, norm_gains, shift_rows, head_shift, expand_shift):
    rows_in, segment = group_pair
    normed = low(layer_norm(rows_in, norm_gains[0], shift_rows[0]))
    mixed_all = product(normed, in_low.reshape(D, 3 * D)).reshape(ROWS_GRP, 3, D)
    queries = low(low_back(mixed_all[:, 0] + head_shift[0]))
    key_rows = low(low_back(mixed_all[:, 1]))
    value_rows = low(low_back(mixed_all[:, 2] + head_shift[1]))
    attended = low(low_back(attention(queries, key_rows, value_rows, segment)))
    middle = rows_in + low_back(product(attended, out_low)) + shift_rows[2]
    normed_two = low(layer_norm(middle, norm_gains[1], shift_rows[1]))
    before = low_back(product(normed_two, expand_low) + expand_shift)
    hidden = low(jax.nn.gelu(before, approximate=False))
    result = middle + product(hidden, shrink_low) + shift_rows[3]
    return jnp.where((segment >= 0)[:, None], result, 0.0)

def forward(inputs_all, project_in, project_out, expand_weight, shrink_weight, norm_gains, shift_rows, head_shift, expand_shift, segments):
    in_low = low(project_in)
    out_low = low(project_out)
    expand_low = low(expand_weight)
    shrink_low = low(shrink_weight)

    def run_group(group_pair):
        return group_forward(group_pair, in_low, out_low, expand_low, shrink_low, norm_gains, shift_rows, head_shift, expand_shift)
    outputs = lax.map(jax.checkpoint(run_group), (inputs_all.reshape(N_DP, ROWS_GRP, D), segments))
    return outputs.reshape(N_DP * ROWS_GRP, D)

def orthogonalize(moment, by_columns):
    scaled = low(moment / (jnp.sqrt(jnp.sum(moment * moment)) + 1e-07))
    for sweep_index in range(NS_ITERS):
        if by_columns:
            gram = low(product(scaled, scaled.T))
            first_term = product(gram, scaled)
            following = coef_a * scaled + coef_b * first_term + coef_c * product(gram, low(first_term))
        else:
            gram = low(product(scaled.T, scaled))
            first_term = product(scaled, gram)
            following = coef_a * scaled + coef_b * first_term + coef_c * product(low(first_term), gram)
        if sweep_index + 1 < NS_ITERS:
            scaled = low(following)
        else:
            scaled = following
    return scaled

def reference(patches, cotangent, item_group, item_length, project_in, project_out, expand_weight, shrink_weight, moment_in, moment_out, moment_expand, moment_shrink, norm_gains, shift_rows, head_shift, expand_shift, moment_gains, moment_shifts, moment_head, moment_expand_shift):
    segments = jax.vmap(group_segments, in_axes=(None, None, 0))(item_group, item_length, jnp.arange(N_DP, dtype=jnp.int32))
    forward_fn = partial(forward, segments=segments)
    block_value, pull_back = jax.vjp(forward_fn, patches.astype(jnp.float32), project_in, project_out, expand_weight, shrink_weight, norm_gains, shift_rows, head_shift, expand_shift)
    grads = pull_back(cotangent.astype(jnp.float32))
    grad_patch, grad_in, grad_out, grad_expand, grad_shrink, grad_gains, grad_shifts, grad_head, grad_expand_shift = grads
    block_out = block_value.astype(jnp.bfloat16)
    patch_grad = grad_patch.astype(jnp.bfloat16)
    next_moment_in = muon_decay * moment_in + grad_in
    next_moment_out = muon_decay * moment_out + grad_out
    next_moment_expand = muon_decay * moment_expand + grad_expand
    next_moment_shrink = muon_decay * moment_shrink + grad_shrink
    orth_in = orthogonalize(next_moment_in.reshape(D, 3 * D), True).reshape(D, 3, D)
    orth_out = orthogonalize(next_moment_out, False)
    orth_expand = orthogonalize(next_moment_expand, True)
    orth_shrink = orthogonalize(next_moment_shrink, False)
    next_in = project_in - 1.25 * orth_in
    next_out = project_out - 2.0 * orth_out
    next_expand = expand_weight - 1.0 * orth_expand
    next_shrink = shrink_weight - 0.5 * orth_shrink
    vector_rate = 0.2 / jnp.sqrt(jnp.float32(TOKENS))
    next_moment_gains = plain_decay * moment_gains + grad_gains
    next_moment_shifts = plain_decay * moment_shifts + grad_shifts
    next_moment_head = plain_decay * moment_head + grad_head
    next_moment_expand_shift = plain_decay * moment_expand_shift + grad_expand_shift
    next_gains = norm_gains - vector_rate * next_moment_gains
    next_shifts = shift_rows - vector_rate * next_moment_shifts
    next_head_shift = head_shift - vector_rate * next_moment_head
    next_expand_shift = expand_shift - vector_rate * next_moment_expand_shift
    return (block_out, patch_grad, next_in, next_out, next_expand, next_shrink, next_in.astype(jnp.bfloat16), next_out.astype(jnp.bfloat16), next_expand.astype(jnp.bfloat16), next_shrink.astype(jnp.bfloat16), next_moment_in, next_moment_out, next_moment_expand, next_moment_shrink, next_gains, next_shifts, next_head_shift, next_expand_shift, next_moment_gains, next_moment_shifts, next_moment_head, next_moment_expand_shift)
```

```python
from functools import partial
import math

import jax
import jax.numpy as jnp
from jax import lax
from jax.experimental import pallas as pl
from jax.experimental.pallas import tpu as pltpu
from jax.sharding import PartitionSpec as P

D = 1024
HD = 64
FF = 4096
ROWS_GRP = 2048
NS_ITERS = 5


norm_eps = 1e-06
coef_a = 3.4445
coef_b = -4.775
coef_c = 2.0315
muon_decay = 0.95
plain_decay = 0.5
neg_fill = -1e30


def layer_norm(values, scale_row, shift_row):
    row_mean = jnp.mean(values, axis=-1, keepdims=True)
    centered = values - row_mean
    spread = jnp.mean(centered * centered, axis=-1, keepdims=True)
    return centered * lax.rsqrt(spread + norm_eps) * scale_row + shift_row


def group_segments(item_group, item_length, group_index):
    member = item_group == group_index
    lengths = jnp.where(member, item_length, 0)
    item_ends = jnp.cumsum(lengths)
    item_starts = item_ends - lengths
    row_ids = jnp.arange(ROWS_GRP, dtype=jnp.int32)[:, None]
    inside = (row_ids >= item_starts[None, :]) & (row_ids < item_ends[None, :]) & member[None, :]
    labels = jnp.arange(item_group.shape[0], dtype=jnp.int32)[None, :]
    return jnp.max(jnp.where(inside, labels, -1), axis=1)


MESH = pl.DeviceIdType.MESH
CUT = 256
STRIPS = D // CUT
STARTS = [sum(D - CUT * i for i in range(k)) for k in range(STRIPS + 1)]
PACKED = STARTS[STRIPS]
HALF = PACKED // 2
VMEM_BYTES = 64 * 1024 * 1024 - 65536


def in_vmem(count):
    return [pl.BlockSpec(memory_space=pltpu.VMEM)] * count


def nt_dot(left, right):
    return lax.dot_general(
        left, right, (((1,), (1,)), ((), ())), preferred_element_type=jnp.float32
    )


def tn_dot(left, right):
    return lax.dot_general(
        left, right, (((0,), (0,)), ((), ())), preferred_element_type=jnp.float32
    )


def gram_kernel(in_ref, out_ref, expand_ref, shrink_ref, gram_ref):
    for slot, ref, by_columns in (
        (0, in_ref, True),
        (1, out_ref, False),
        (2, expand_ref, True),
        (3, shrink_ref, False),
    ):
        for i in range(STRIPS):
            if by_columns:
                strip = nt_dot(ref[i * CUT : (i + 1) * CUT, :], ref[i * CUT :, :])
            else:
                strip = tn_dot(ref[:, i * CUT : (i + 1) * CUT], ref[:, i * CUT :])
            gram_ref[slot, :, STARTS[i] : STARTS[i + 1]] = strip


def gram_strips(low_in, low_out, low_expand, low_shrink):
    return pl.pallas_call(
        gram_kernel,
        out_shape=jax.ShapeDtypeStruct((4, CUT, PACKED), jnp.float32),
        in_specs=in_vmem(4),
        out_specs=in_vmem(1)[0],
        compiler_params=pltpu.CompilerParams(vmem_limit_bytes=VMEM_BYTES),
        name="gram_strips",
    )(low_in, low_out, low_expand, low_shrink)


def places():
    model = lax.axis_index("mp")
    return lax.axis_index("dp"), model // 2, model % 2


def greet(peers):
    barrier = pltpu.get_barrier_semaphore()
    for peer in peers:
        pl.semaphore_signal(barrier, inc=1, device_id=peer, device_id_type=MESH)
    pl.semaphore_wait(barrier, len(peers))


def gram_exchange_kernel(
    chips, gram_ref, own_ref, chip_ref, core_ref, far_ref, core_send, core_recv, far_send, far_recv, row_send, row_recv
):
    row, chip, core = places()
    mine = chip % 2
    half = row % 2
    greet(
        [(row, chip * 2 + 1 - core), (row + 1 - 2 * half, chip * 2 + core)]
        + [(row, lax.rem(chip + step, chips) * 2 + core) for step in range(1, chips)]
    )
    core_copies = []
    for k in range(2):
        copy = pltpu.make_async_remote_copy(
            src_ref=gram_ref.at[2 * k + 1 - core],
            dst_ref=core_ref.at[k],
            send_sem=core_send.at[k],
            recv_sem=core_recv.at[k],
            device_id=(row, chip * 2 + 1 - core),
            device_id_type=MESH,
        )
        copy.start()
        core_copies.append(copy)
    for copy in core_copies:
        copy.wait()
    for k in range(2):
        chip_ref[k] = gram_ref[2 * k + core] + core_ref[k]
    far_copies = []
    for step in range(1, chips):
        other = lax.rem(chip + step, chips)
        copy = pltpu.make_async_remote_copy(
            src_ref=chip_ref.at[other % 2, :, pl.ds(pl.multiple_of(half * HALF, 128), HALF)],
            dst_ref=far_ref.at[step - 1, :, pl.ds(pl.multiple_of(half * HALF, 128), HALF)],
            send_sem=far_send.at[step - 1],
            recv_sem=far_recv.at[step - 1],
            device_id=(row, other * 2 + core),
            device_id_type=MESH,
        )
        copy.start()
        far_copies.append(copy)
    row_copies = []
    for step in range(1, chips):
        far_copies[step - 1].wait_recv()
        copy = pltpu.make_async_remote_copy(
            src_ref=far_ref.at[step - 1, :, pl.ds(pl.multiple_of(half * HALF, 128), HALF)],
            dst_ref=far_ref.at[step - 1, :, pl.ds(pl.multiple_of(half * HALF, 128), HALF)],
            send_sem=row_send.at[step - 1],
            recv_sem=row_recv.at[step - 1],
            device_id=(row + 1 - 2 * half, chip * 2 + core),
            device_id_type=MESH,
        )
        copy.start()
        row_copies.append(copy)
    for copy in far_copies:
        copy.wait_send()
    for copy in row_copies:
        copy.wait()
    total = chip_ref[mine]
    for step in range(1, chips):
        total = total + far_ref[step - 1]
    own_ref[...] = total


def gram_exchange(grams):
    chips = lax.axis_size("mp") // 2
    shape = (CUT, PACKED)
    return pl.pallas_call(
        partial(gram_exchange_kernel, chips),
        out_shape=jax.ShapeDtypeStruct(shape, jnp.float32),
        in_specs=in_vmem(1),
        out_specs=in_vmem(1)[0],
        scratch_shapes=[
            pltpu.VMEM((2,) + shape, jnp.float32),
            pltpu.VMEM((2,) + shape, jnp.float32),
            pltpu.VMEM((chips - 1,) + shape, jnp.float32),
            pltpu.SemaphoreType.DMA((2,)),
            pltpu.SemaphoreType.DMA((2,)),
            pltpu.SemaphoreType.DMA((chips - 1,)),
            pltpu.SemaphoreType.DMA((chips - 1,)),
            pltpu.SemaphoreType.DMA((chips - 1,)),
            pltpu.SemaphoreType.DMA((chips - 1,)),
        ],
        compiler_params=pltpu.CompilerParams(
            collective_id=1, has_side_effects=True, vmem_limit_bytes=VMEM_BYTES
        ),
        name="gram_exchange",
    )(grams)


BLOCK = 512


def chain_kernel(gram_ref, factor_ref, high, rest, inner, gram, first, first_low):
    for i in range(STRIPS):
        for j in range(i, STRIPS):
            start = STARTS[i] + (j - i) * CUT
            block = gram_ref[:, start : start + CUT]
            block_high = block.astype(jnp.bfloat16)
            block_rest = (block - block_high.astype(jnp.float32)).astype(jnp.bfloat16)
            high[i * CUT : (i + 1) * CUT, j * CUT : (j + 1) * CUT] = block_high
            rest[i * CUT : (i + 1) * CUT, j * CUT : (j + 1) * CUT] = block_rest
            if j > i:
                high[j * CUT : (j + 1) * CUT, i * CUT : (i + 1) * CUT] = block_high.T
                rest[j * CUT : (j + 1) * CUT, i * CUT : (i + 1) * CUT] = block_rest.T

    def rows_of(index):
        return pl.ds(pl.multiple_of(index * BLOCK, BLOCK), BLOCK)

    def product(left, right):
        return jnp.dot(left, right, preferred_element_type=jnp.float32)

    @pl.loop(0, D // BLOCK)
    def _(index):
        rows = rows_of(index)
        row_ids = lax.broadcasted_iota(jnp.int32, (BLOCK, D), 0) + index * BLOCK
        eye = (row_ids == lax.broadcasted_iota(jnp.int32, (BLOCK, D), 1)).astype(jnp.float32)
        second = product(high[rows, :], high[...])
        following = coef_a * eye + coef_b * high[rows, :].astype(jnp.float32) + coef_c * second
        factor_ref[rows, :] = following.astype(jnp.bfloat16)

    @pl.loop(1, NS_ITERS)
    def _(sweep):
        @pl.loop(0, D // BLOCK)
        def _(index):
            rows = rows_of(index)
            inner[rows, :] = (
                nt_dot(high[rows, :], factor_ref[...]) + nt_dot(rest[rows, :], factor_ref[...])
            ).astype(jnp.bfloat16)

        @pl.loop(0, D // BLOCK)
        def _(index):
            rows = rows_of(index)
            block = product(factor_ref[rows, :], inner[...]).astype(jnp.bfloat16)
            gram[rows, :] = block
            term = product(block, factor_ref[...])
            first[rows, :] = term
            first_low[rows, :] = term.astype(jnp.bfloat16)

        @pl.loop(0, D // BLOCK)
        def _(index):
            rows = rows_of(index)
            second = product(gram[rows, :], first_low[...])
            following = (
                coef_a * factor_ref[rows, :].astype(jnp.float32)
                + coef_b * first[rows, :]
                + coef_c * second
            )
            factor_ref[rows, :] = following.astype(jnp.bfloat16)


def sweep_chain(own_gram):
    low = pltpu.VMEM((D, D), jnp.bfloat16)
    return pl.pallas_call(
        chain_kernel,
        out_shape=jax.ShapeDtypeStruct((D, D), jnp.bfloat16),
        in_specs=in_vmem(1),
        out_specs=in_vmem(1)[0],
        scratch_shapes=[low, low, low, low, pltpu.VMEM((D, D), jnp.float32), low],
        compiler_params=pltpu.CompilerParams(vmem_limit_bytes=VMEM_BYTES),
        name="sweep_chain",
    )(own_gram)


def factor_exchange_kernel(own_ref, all_ref, far_ref, local_sem, send_sem, recv_sem):
    row, chip, core = places()
    mine = chip % 2
    half = row % 2
    away = chip + 1 - 2 * mine
    greet(
        [
            (row, chip * 2 + 1 - core),
            (row + 1 - 2 * half, chip * 2 + core),
            (row, away * 2 + core),
        ]
    )
    rows = pl.ds(pl.multiple_of(half * (D // 2), 128), D // 2)

    def remote(src, dst, index, peer):
        return pltpu.make_async_remote_copy(
            src_ref=src,
            dst_ref=dst,
            send_sem=send_sem.at[index],
            recv_sem=recv_sem.at[index],
            device_id=peer,
            device_id_type=MESH,
        )

    across = remote(own_ref.at[rows, :], far_ref.at[rows, :], 0, (row, away * 2 + core))
    across.start()
    beside = remote(
        own_ref, all_ref.at[2 * mine + core], 1, (row, chip * 2 + 1 - core)
    )
    beside.start()
    keep = pltpu.make_async_copy(own_ref, all_ref.at[2 * mine + core], local_sem.at[0])
    keep.start()
    across.wait()
    along = remote(
        far_ref.at[rows, :], far_ref.at[rows, :], 2, (row + 1 - 2 * half, chip * 2 + core)
    )
    along.start()
    along.wait()
    onward = remote(
        far_ref, all_ref.at[2 * (1 - mine) + core], 3, (row, chip * 2 + 1 - core)
    )
    onward.start()
    keep_far = pltpu.make_async_copy(far_ref, all_ref.at[2 * (1 - mine) + core], local_sem.at[1])
    keep_far.start()
    beside.wait()
    onward.wait()
    keep.wait()
    keep_far.wait()


def factor_exchange(factor):
    return pl.pallas_call(
        factor_exchange_kernel,
        out_shape=jax.ShapeDtypeStruct((4, D, D), jnp.bfloat16),
        in_specs=in_vmem(1),
        out_specs=in_vmem(1)[0],
        scratch_shapes=[
            pltpu.VMEM((D, D), jnp.bfloat16),
            pltpu.SemaphoreType.DMA((2,)),
            pltpu.SemaphoreType.DMA((4,)),
            pltpu.SemaphoreType.DMA((4,)),
        ],
        compiler_params=pltpu.CompilerParams(
            collective_id=2, has_side_effects=True, vmem_limit_bytes=VMEM_BYTES
        ),
        name="factor_exchange",
    )(factor)


def on_device(
    patches,
    cotangent,
    item_group,
    item_length,
    project_in,
    project_out,
    expand_weight,
    shrink_weight,
    moment_in,
    moment_out,
    moment_expand,
    moment_shrink,
    norm_gains,
    shift_rows,
    head_shift,
    expand_shift,
    moment_gains,
    moment_shifts,
    moment_head,
    moment_expand_shift,
):
    dp_count = lax.axis_size("dp")
    group_index = lax.axis_index("dp")
    model_index = lax.axis_index("mp")
    own_rows = patches.shape[0]
    local_width = project_out.shape[0]
    local_heads = local_width // HD
    local_hidden = shrink_weight.shape[0]
    segment = group_segments(item_group, item_length, group_index)
    own_segment = lax.dynamic_slice_in_dim(segment, model_index * own_rows, own_rows, 0)
    live_rows = (own_segment >= 0)[:, None]
    patch_values = patches.astype(jnp.float32)
    normed, norm_one_back = jax.vjp(layer_norm, patch_values, norm_gains[0], shift_rows[0])
    normed_all = lax.all_gather(normed.astype(jnp.bfloat16), "mp", axis=0, tiled=True)
    in_low = project_in.astype(jnp.bfloat16).reshape(D, 3 * local_width)
    mixed_all = jnp.dot(normed_all, in_low, preferred_element_type=jnp.float32).reshape(
        ROWS_GRP, 3, local_width
    )
    queries = (
        (mixed_all[:, 0] + head_shift[0]).astype(jnp.bfloat16).reshape(ROWS_GRP, local_heads, HD)
    )
    key_rows = mixed_all[:, 1].astype(jnp.bfloat16).reshape(ROWS_GRP, local_heads, HD)
    value_rows = (
        (mixed_all[:, 2] + head_shift[1]).astype(jnp.bfloat16).reshape(ROWS_GRP, local_heads, HD)
    )
    block_rows = min(512, ROWS_GRP)
    block_count = ROWS_GRP // block_rows
    score_scale = HD ** (-0.5)

    def block_scores(block_index):
        row_start = block_index * block_rows
        q_block = lax.dynamic_slice_in_dim(queries, row_start, block_rows, 0)
        seg_block = lax.dynamic_slice_in_dim(segment, row_start, block_rows, 0)
        scores = (
            jnp.einsum("qhe,khe->hqk", q_block, key_rows, preferred_element_type=jnp.float32)
            * score_scale
        )
        allowed = (seg_block[:, None] == segment[None, :])[None]
        return (jnp.where(allowed, scores, neg_fill), q_block)

    def attend_block(block_index):
        scores, q_block = block_scores(block_index)
        top_score = jnp.max(scores, axis=-1, keepdims=True)
        exp_scores = jnp.exp(scores - top_score)
        row_total = jnp.sum(exp_scores, axis=-1, keepdims=True)
        weights = (exp_scores / row_total).astype(jnp.bfloat16)
        attended = jnp.einsum(
            "hqk,khe->qhe", weights, value_rows, preferred_element_type=jnp.float32
        )
        return (attended, top_score[..., 0] + jnp.log(row_total[..., 0]))

    attended, log_totals = lax.map(attend_block, jnp.arange(block_count))
    attended_low = attended.reshape(ROWS_GRP, local_width).astype(jnp.bfloat16)
    out_low = project_out.astype(jnp.bfloat16)
    row_block = attended_low
    attn_part = lax.psum_scatter(
        jnp.dot(row_block, out_low, preferred_element_type=jnp.float32).astype(jnp.bfloat16),
        "mp",
        scatter_dimension=0,
        tiled=True,
    ).astype(jnp.float32)
    middle = patch_values + attn_part + shift_rows[2]
    normed_two, norm_two_back = jax.vjp(layer_norm, middle, norm_gains[1], shift_rows[1])
    normed_low = normed_two.astype(jnp.bfloat16)
    gelu_exact = partial(jax.nn.gelu, approximate=False)
    out_grad = jnp.where(live_rows, cotangent, jnp.zeros_like(cotangent))
    normed_two_all = lax.all_gather(normed_low, "mp", axis=0, tiled=True)
    expand_low = expand_weight.astype(jnp.bfloat16)
    shrink_low = shrink_weight.astype(jnp.bfloat16)
    shift_part = lax.dynamic_slice_in_dim(expand_shift, model_index * local_hidden, local_hidden, 0)
    before = jnp.dot(normed_two_all, expand_low, preferred_element_type=jnp.float32) + shift_part
    hidden, gelu_back = jax.vjp(gelu_exact, before)
    hidden_low = hidden.astype(jnp.bfloat16)
    row_block = lax.slice_in_dim(hidden_low, 0, own_rows * lax.axis_size("mp"), axis=0)
    ffn_part = lax.psum_scatter(
        jnp.dot(row_block, shrink_low, preferred_element_type=jnp.float32).astype(jnp.bfloat16),
        "mp",
        scatter_dimension=0,
        tiled=True,
    ).astype(jnp.float32)
    block_value = middle + ffn_part + shift_rows[3]
    out_grad_all = lax.all_gather(out_grad, "mp", axis=0, tiled=True)
    grad_shrink = jnp.einsum(
        "rf,rd->fd", hidden_low, out_grad_all, preferred_element_type=jnp.float32
    )
    grad_hidden = jnp.einsum(
        "rd,fd->rf", out_grad_all, shrink_low, preferred_element_type=jnp.float32
    )
    grad_before = gelu_back(grad_hidden)[0].astype(jnp.bfloat16)
    grad_expand = jnp.einsum(
        "rd,rf->df", normed_two_all, grad_before, preferred_element_type=jnp.float32
    )
    shift_sum = jnp.sum(grad_before, axis=0, dtype=jnp.float32)
    grad_expand_shift = lax.dynamic_update_slice_in_dim(
        jnp.zeros((FF,), jnp.float32), shift_sum, model_index * local_hidden, 0
    )
    row_block = grad_before
    grad_normed_two = lax.psum_scatter(
        jnp.einsum("rf,df->rd", row_block, expand_low, preferred_element_type=jnp.float32).astype(
            jnp.bfloat16
        ),
        "mp",
        scatter_dimension=0,
        tiled=True,
    ).astype(jnp.float32)
    block_out = jnp.where(live_rows, block_value, 0.0).astype(jnp.bfloat16)
    grad_middle_norm, gain_two_grad, shift_two_grad = norm_two_back(grad_normed_two)
    out_grad_values = out_grad.astype(jnp.float32)
    grad_middle = out_grad_values + grad_middle_norm
    middle_all = lax.all_gather(grad_middle.astype(jnp.bfloat16), "mp", axis=0, tiled=True)
    grad_out = jnp.einsum("rc,rd->cd", attended_low, middle_all, preferred_element_type=jnp.float32)
    grad_attended = jnp.einsum("rd,cd->rc", middle_all, out_low, preferred_element_type=jnp.float32)
    grad_attended = grad_attended.astype(jnp.bfloat16).reshape(ROWS_GRP, local_heads, HD)

    def back_block(carry_pair, block_index):
        key_grad, value_grad = carry_pair
        scores, q_block = block_scores(block_index)
        probs = jnp.exp(scores - log_totals[block_index][..., None])
        grad_block = lax.dynamic_slice_in_dim(
            grad_attended, block_index * block_rows, block_rows, 0
        )
        grad_probs = jnp.einsum(
            "qhe,khe->hqk", grad_block, value_rows, preferred_element_type=jnp.float32
        )
        inner_sum = jnp.sum(probs * grad_probs, axis=-1, keepdims=True)
        grad_scores = (probs * (grad_probs - inner_sum)).astype(jnp.bfloat16)
        query_grad = (
            jnp.einsum("hqk,khe->qhe", grad_scores, key_rows, preferred_element_type=jnp.float32)
            * score_scale
        )
        key_grad = (
            key_grad
            + jnp.einsum("hqk,qhe->khe", grad_scores, q_block, preferred_element_type=jnp.float32)
            * score_scale
        )
        value_grad = value_grad + jnp.einsum(
            "hqk,qhe->khe",
            probs.astype(jnp.bfloat16),
            grad_block,
            preferred_element_type=jnp.float32,
        )
        return ((key_grad, value_grad), query_grad)

    zero_grads = jnp.zeros((ROWS_GRP, local_heads, HD), jnp.float32)
    (key_grad, value_grad), query_grad = lax.scan(
        back_block, (zero_grads, zero_grads), jnp.arange(block_count)
    )
    grad_mixed = jnp.stack(
        [
            query_grad.reshape(ROWS_GRP, local_width),
            key_grad.reshape(ROWS_GRP, local_width),
            value_grad.reshape(ROWS_GRP, local_width),
        ],
        axis=1,
    ).astype(jnp.bfloat16)
    grad_mixed_flat = grad_mixed.reshape(ROWS_GRP, 3 * local_width)
    grad_in = jnp.einsum(
        "rd,rc->dc", normed_all, grad_mixed_flat, preferred_element_type=jnp.float32
    )
    grad_head = jnp.stack(
        [
            jnp.sum(grad_mixed[:, 0], axis=0, dtype=jnp.float32),
            jnp.sum(grad_mixed[:, 2], axis=0, dtype=jnp.float32),
        ]
    )
    row_block = grad_mixed_flat
    grad_normed_one = lax.psum_scatter(
        jnp.einsum("rc,dc->rd", row_block, in_low, preferred_element_type=jnp.float32).astype(
            jnp.bfloat16
        ),
        "mp",
        scatter_dimension=0,
        tiled=True,
    ).astype(jnp.float32)
    grad_patch_norm, gain_one_grad, shift_one_grad = norm_one_back(grad_normed_one)
    patch_grad = (grad_middle + grad_patch_norm).astype(jnp.bfloat16)
    gain_grads = jnp.stack([gain_one_grad, gain_two_grad])
    shift_grads = jnp.stack(
        [
            shift_one_grad,
            shift_two_grad,
            jnp.sum(grad_middle, axis=0),
            jnp.sum(out_grad_values, axis=0),
        ]
    )
    summed_in, summed_out, summed_expand, summed_shrink, summed_head = (
        lax.psum(grad_in.astype(jnp.bfloat16), "dp").astype(jnp.float32),
        lax.psum(grad_out.astype(jnp.bfloat16), "dp").astype(jnp.float32),
        lax.psum(grad_expand.astype(jnp.bfloat16), "dp").astype(jnp.float32),
        lax.psum(grad_shrink.astype(jnp.bfloat16), "dp").astype(jnp.float32),
        lax.psum(grad_head.astype(jnp.bfloat16), "dp").astype(jnp.float32),
    )
    next_moment_in = muon_decay * moment_in + summed_in.reshape(D, 3, local_width)
    next_moment_out = muon_decay * moment_out + summed_out
    next_moment_expand = muon_decay * moment_expand + summed_expand
    next_moment_shrink = muon_decay * moment_shrink + summed_shrink
    matrices = [
        next_moment_in.reshape(D, 3 * local_width),
        next_moment_out,
        next_moment_expand,
        next_moment_shrink,
    ]
    orient = [True, False, True, False]
    square_sums = jnp.stack([jnp.sum(matrix * matrix) for matrix in matrices])
    square_total = lax.psum(square_sums, "mp")
    gain_total, shift_total, expand_shift_total = lax.psum(
        (gain_grads, shift_grads, grad_expand_shift), ("dp", "mp")
    )
    scaled = []
    for matrix_index in range(4):
        factor = 1.0 / (jnp.sqrt(square_total[matrix_index]) + 1e-07)
        scaled.append((matrices[matrix_index] * factor).astype(jnp.bfloat16))
    factors = factor_exchange(sweep_chain(gram_exchange(gram_strips(*scaled))))
    scaled = [
        jnp.dot(factors[index], scaled[index], preferred_element_type=jnp.float32)
        if orient[index]
        else jnp.einsum("rc,dc->rd", scaled[index], factors[index], preferred_element_type=jnp.float32)
        for index in range(4)
    ]
    next_in = project_in - 1.25 * scaled[0].reshape(D, 3, local_width)
    next_out = project_out - 2.0 * scaled[1]
    next_expand = expand_weight - 1.0 * scaled[2]
    next_shrink = shrink_weight - 0.5 * scaled[3]
    vector_rate = 0.2 / math.sqrt(ROWS_GRP * dp_count)
    next_moment_gains = plain_decay * moment_gains + gain_total
    next_moment_shifts = plain_decay * moment_shifts + shift_total
    next_moment_head = plain_decay * moment_head + summed_head
    next_moment_expand_shift = plain_decay * moment_expand_shift + expand_shift_total
    next_gains = norm_gains - vector_rate * next_moment_gains
    next_shifts = shift_rows - vector_rate * next_moment_shifts
    next_head_shift = head_shift - vector_rate * next_moment_head
    next_expand_shift = expand_shift - vector_rate * next_moment_expand_shift
    return (
        block_out,
        patch_grad,
        next_in,
        next_out,
        next_expand,
        next_shrink,
        next_in.astype(jnp.bfloat16),
        next_out.astype(jnp.bfloat16),
        next_expand.astype(jnp.bfloat16),
        next_shrink.astype(jnp.bfloat16),
        next_moment_in,
        next_moment_out,
        next_moment_expand,
        next_moment_shrink,
        next_gains,
        next_shifts,
        next_head_shift,
        next_expand_shift,
        next_moment_gains,
        next_moment_shifts,
        next_moment_head,
        next_moment_expand_shift,
    )


def solution(mesh):
    placed = (
        P(("dp", "mp"), None),
        P(("dp", "mp"), None),
        P(),
        P(),
        P(None, None, "mp"),
        P("mp", None),
        P(None, "mp"),
        P("mp", None),
        P(None, None, "mp"),
        P("mp", None),
        P(None, "mp"),
        P("mp", None),
        P(),
        P(),
        P(None, "mp"),
        P(),
        P(),
        P(),
        P(None, "mp"),
        P(),
    )
    return jax.shard_map(
        on_device,
        mesh=mesh,
        in_specs=placed,
        out_specs=(
            P(("dp", "mp"), None),
            P(("dp", "mp"), None),
            P(None, None, "mp"),
            P("mp", None),
            P(None, "mp"),
            P("mp", None),
            P(None, None, "mp"),
            P("mp", None),
            P(None, "mp"),
            P("mp", None),
            P(None, None, "mp"),
            P("mp", None),
            P(None, "mp"),
            P("mp", None),
            P(),
            P(),
            P(None, "mp"),
            P(),
            P(),
            P(),
            P(None, "mp"),
            P(),
        ),
        check_vma=False,
    )
```

```python
from functools import partial
import math

import jax
import jax.numpy as jnp
from jax import lax
from jax.experimental import pallas as pl
from jax.experimental.pallas import tpu as pltpu
from jax.sharding import PartitionSpec as P


D = 1024
HD = 64
FF = 4096
ROWS_GRP = 2048
NS_ITERS = 5


norm_eps = 1e-06
coef_a = 3.4445
coef_b = -4.775
coef_c = 2.0315
muon_decay = 0.95
plain_decay = 0.5
neg_fill = -1e30


def layer_norm(values, scale_row, shift_row):
    row_mean = jnp.mean(values, axis=-1, keepdims=True)
    centered = values - row_mean
    spread = jnp.mean(centered * centered, axis=-1, keepdims=True)
    return centered * lax.rsqrt(spread + norm_eps) * scale_row + shift_row


def group_spans(item_group, item_length, group_index):
    member = item_group == group_index
    lengths = jnp.where(member, item_length, 0)
    item_ends = jnp.cumsum(lengths)
    item_starts = item_ends - lengths
    row_ids = jnp.arange(ROWS_GRP, dtype=jnp.int32)[:, None]
    inside = (row_ids >= item_starts[None, :]) & (row_ids < item_ends[None, :]) & member[None, :]
    used = item_ends[-1]
    live = row_ids[:, 0] < used
    first = jnp.where(live, jnp.max(jnp.where(inside, item_starts[None, :], 0), axis=1), used)
    last = jnp.where(live, jnp.max(jnp.where(inside, item_ends[None, :], 0), axis=1), ROWS_GRP)
    return used, first.astype(jnp.int32), last.astype(jnp.int32)


MESH = pl.DeviceIdType.MESH
CUT = 256
STRIPS = D // CUT
PAIRS = [(i, j) for i in range(STRIPS) for j in range(i, STRIPS)]
COUNT = len(PAIRS)
HALF = COUNT // 2
BLOCK = 512
VMEM_BYTES = 64 * 1024 * 1024 - 65536


def in_vmem(count):
    return [pl.BlockSpec(memory_space=pltpu.VMEM)] * count


def nt_dot(left, right):
    return lax.dot_general(
        left, right, (((1,), (1,)), ((), ())), preferred_element_type=jnp.float32
    )


def tn_dot(left, right):
    return lax.dot_general(
        left, right, (((0,), (0,)), ((), ())), preferred_element_type=jnp.float32
    )


def gram_kernel(in_ref, out_ref, expand_ref, shrink_ref, gram_ref):
    for slot, ref, by_columns in (
        (0, in_ref, True),
        (1, out_ref, False),
        (2, expand_ref, True),
        (3, shrink_ref, False),
    ):
        for i in range(STRIPS):
            if by_columns:
                strip = nt_dot(ref[i * CUT : (i + 1) * CUT, :], ref[i * CUT :, :])
            else:
                strip = tn_dot(ref[:, i * CUT : (i + 1) * CUT], ref[:, i * CUT :])
            for j in range(i, STRIPS):
                gram_ref[slot, PAIRS.index((i, j))] = strip[:, (j - i) * CUT : (j - i + 1) * CUT]


def gram_strips(low_in, low_out, low_expand, low_shrink):
    return pl.pallas_call(
        gram_kernel,
        out_shape=jax.ShapeDtypeStruct((4, COUNT, CUT, CUT), jnp.float32),
        in_specs=in_vmem(4),
        out_specs=in_vmem(1)[0],
        compiler_params=pltpu.CompilerParams(vmem_limit_bytes=VMEM_BYTES),
        name="gram_strips",
    )(low_in, low_out, low_expand, low_shrink)


def places():
    model = lax.axis_index("mp")
    return lax.axis_index("dp"), model // 2, model % 2


def greet(peers):
    barrier = pltpu.get_barrier_semaphore()
    for peer in peers:
        pl.semaphore_signal(barrier, inc=1, device_id=peer, device_id_type=MESH)
    pl.semaphore_wait(barrier, len(peers))


def remote(src, dst, send_sem, recv_sem, peer):
    return pltpu.make_async_remote_copy(
        src_ref=src,
        dst_ref=dst,
        send_sem=send_sem,
        recv_sem=recv_sem,
        device_id=peer,
        device_id_type=MESH,
    )


def gram_exchange_kernel(
    chips,
    gram_ref,
    own_ref,
    chip_ref,
    core_ref,
    far_ref,
    near_send,
    near_recv,
    core_send,
    core_recv,
    far_send,
    far_recv,
    row_send,
    row_recv,
):
    row, chip, core = places()
    mine = chip % 2
    theirs = 1 - mine
    half = row % 2
    beside = (row, chip * 2 + 1 - core)
    along = (row + 1 - 2 * half, chip * 2 + core)
    greet(
        [beside, along]
        + [(row, lax.rem(chip + step, chips) * 2 + core) for step in range(1, chips)]
    )
    near = [
        remote(
            gram_ref.at[2 * theirs + 1 - core, half * HALF + b],
            core_ref.at[theirs, half * HALF + b],
            near_send.at[b],
            near_recv.at[b],
            beside,
        )
        for b in range(HALF)
    ]
    kept = remote(
        gram_ref.at[2 * mine + 1 - core], core_ref.at[mine], core_send.at[0], core_recv.at[0], beside
    )
    for copy in near:
        copy.start()
    kept.start()
    far = {}

    def send_far(step, b):
        other = lax.rem(chip + step, chips)
        far[step, b] = remote(
            chip_ref.at[other % 2, half * HALF + b],
            far_ref.at[step - 1, half * HALF + b],
            far_send.at[step - 1, b],
            far_recv.at[step - 1, b],
            (row, other * 2 + core),
        )
        far[step, b].start()

    for b in range(HALF):
        near[b].wait()
        place = half * HALF + b
        chip_ref[theirs, place] = gram_ref[2 * theirs + core, place] + core_ref[theirs, place]
        for step in range(1, chips, 2):
            send_far(step, b)
    kept.wait()
    chip_ref[mine] = gram_ref[2 * mine + core] + core_ref[mine]
    for step in range(2, chips, 2):
        for b in range(HALF):
            send_far(step, b)
    onward = []
    for step in range(1, chips):
        for b in range(HALF):
            far[step, b].wait_recv()
            copy = remote(
                far_ref.at[step - 1, half * HALF + b],
                far_ref.at[step - 1, half * HALF + b],
                row_send.at[step - 1, b],
                row_recv.at[step - 1, b],
                along,
            )
            copy.start()
            onward.append(copy)
    for copy in far.values():
        copy.wait_send()
    for copy in onward:
        copy.wait()
    total = chip_ref[mine]
    for step in range(1, chips):
        total = total + far_ref[step - 1]
    own_ref[...] = total


def gram_exchange(grams):
    chips = lax.axis_size("mp") // 2
    shape = (COUNT, CUT, CUT)
    near = pltpu.SemaphoreType.DMA((HALF,))
    whole = pltpu.SemaphoreType.DMA((1,))
    away = pltpu.SemaphoreType.DMA((chips - 1, HALF))
    return pl.pallas_call(
        partial(gram_exchange_kernel, chips),
        out_shape=jax.ShapeDtypeStruct(shape, jnp.float32),
        in_specs=in_vmem(1),
        out_specs=in_vmem(1)[0],
        scratch_shapes=[
            pltpu.VMEM((2,) + shape, jnp.float32),
            pltpu.VMEM((2,) + shape, jnp.float32),
            pltpu.VMEM((chips - 1,) + shape, jnp.float32),
            near,
            near,
            whole,
            whole,
            away,
            away,
            away,
            away,
        ],
        compiler_params=pltpu.CompilerParams(
            collective_id=1, has_side_effects=True, vmem_limit_bytes=VMEM_BYTES
        ),
        name="gram_exchange",
    )(grams)


def chain_kernel(gram_ref, factor_ref, high, rest, inner, gram, first, first_low):
    rows_in = lax.broadcasted_iota(jnp.int32, (CUT, CUT), 0)
    diagonal = rows_in == lax.broadcasted_iota(jnp.int32, (CUT, CUT), 1)
    trace = jnp.zeros((), jnp.float32)
    for i in range(STRIPS):
        trace = trace + jnp.sum(jnp.where(diagonal, gram_ref[PAIRS.index((i, i))], 0.0))
    scale = 1.0 / (jnp.sqrt(jnp.full((8, 128), trace, jnp.float32)) + 1e-07)
    scale = jnp.max(scale)
    for index, (i, j) in enumerate(PAIRS):
        block = gram_ref[index] * scale * scale
        block_high = block.astype(jnp.bfloat16)
        block_rest = (block - block_high.astype(jnp.float32)).astype(jnp.bfloat16)
        high[i * CUT : (i + 1) * CUT, j * CUT : (j + 1) * CUT] = block_high
        rest[i * CUT : (i + 1) * CUT, j * CUT : (j + 1) * CUT] = block_rest
        if j > i:
            high[j * CUT : (j + 1) * CUT, i * CUT : (i + 1) * CUT] = block_high.T
            rest[j * CUT : (j + 1) * CUT, i * CUT : (i + 1) * CUT] = block_rest.T

    def rows_of(index):
        return pl.ds(pl.multiple_of(index * BLOCK, BLOCK), BLOCK)

    def product(left, right):
        return jnp.dot(left, right, preferred_element_type=jnp.float32)

    @pl.loop(0, D // BLOCK)
    def _(index):
        rows = rows_of(index)
        row_ids = lax.broadcasted_iota(jnp.int32, (BLOCK, D), 0) + index * BLOCK
        eye = (row_ids == lax.broadcasted_iota(jnp.int32, (BLOCK, D), 1)).astype(jnp.float32)
        second = product(high[rows, :], high[...])
        following = coef_a * eye + coef_b * high[rows, :].astype(jnp.float32) + coef_c * second
        factor_ref[rows, :] = following.astype(jnp.bfloat16)

    @pl.loop(1, NS_ITERS)
    def _(sweep):
        last = jnp.where(sweep == NS_ITERS - 1, scale, 1.0)

        @pl.loop(0, D // BLOCK)
        def _(index):
            rows = rows_of(index)
            inner[rows, :] = (
                nt_dot(high[rows, :], factor_ref[...]) + nt_dot(rest[rows, :], factor_ref[...])
            ).astype(jnp.bfloat16)

        @pl.loop(0, D // BLOCK)
        def _(index):
            rows = rows_of(index)
            block = product(factor_ref[rows, :], inner[...]).astype(jnp.bfloat16)
            gram[rows, :] = block
            term = product(block, factor_ref[...])
            first[rows, :] = term
            first_low[rows, :] = term.astype(jnp.bfloat16)

        @pl.loop(0, D // BLOCK)
        def _(index):
            rows = rows_of(index)
            second = product(gram[rows, :], first_low[...])
            following = (
                coef_a * factor_ref[rows, :].astype(jnp.float32)
                + coef_b * first[rows, :]
                + coef_c * second
            )
            factor_ref[rows, :] = (following * last).astype(jnp.bfloat16)


def sweep_chain(own_gram):
    low = pltpu.VMEM((D, D), jnp.bfloat16)
    return pl.pallas_call(
        chain_kernel,
        out_shape=jax.ShapeDtypeStruct((D, D), jnp.bfloat16),
        in_specs=in_vmem(1),
        out_specs=in_vmem(1)[0],
        scratch_shapes=[low, low, low, low, pltpu.VMEM((D, D), jnp.float32), low],
        compiler_params=pltpu.CompilerParams(vmem_limit_bytes=VMEM_BYTES),
        cost_estimate=pl.CostEstimate(
            flops=42 * D**3, bytes_accessed=6 * D * D, transcendentals=0
        ),
        name="sweep_chain",
    )(own_gram)


PIECES = 4
PIECE = D // 2 // PIECES


def factor_exchange_kernel(
    groups,
    models,
    own_ref,
    vector_ref,
    head_ref,
    all_ref,
    vector_out,
    head_out,
    far_ref,
    model_ref,
    group_ref,
    head_group,
    local_sem,
    beside_send,
    beside_recv,
    across_send,
    across_recv,
    along_send,
    along_recv,
    onward_send,
    onward_recv,
    model_send,
    model_recv,
    group_send,
    group_recv,
    head_send,
    head_recv,
):
    row, chip, core = places()
    model = chip * 2 + core
    mine = chip % 2
    half = row % 2
    next_core = (row, chip * 2 + 1 - core)
    next_chip = (row, (chip + 1 - 2 * mine) * 2 + core)
    next_row = (row + 1 - 2 * half, model)
    greet(
        [(row, lax.rem(model + step, models)) for step in range(1, models)]
        + [(lax.rem(row + step, groups), model) for step in range(1, groups)]
    )

    def part(which, piece):
        return pl.ds(pl.multiple_of(which * (D // 2) + piece * PIECE, PIECE), PIECE)

    model_ref[model] = vector_ref[...]
    model_copies = []
    for step in range(1, models):
        copy = remote(
            vector_ref,
            model_ref.at[model],
            model_send.at[step - 1],
            model_recv.at[model],
            (row, lax.rem(model + step, models)),
        )
        copy.start()
        model_copies.append(copy)
    across = []
    for piece in range(PIECES):
        rows = part(half, piece)
        copy = remote(
            own_ref.at[rows, :],
            far_ref.at[rows, :],
            across_send.at[piece],
            across_recv.at[piece],
            next_chip,
        )
        copy.start()
        across.append(copy)
    beside = remote(
        own_ref, all_ref.at[2 * mine + core], beside_send.at[0], beside_recv.at[0], next_core
    )
    beside.start()
    keep = pltpu.make_async_copy(own_ref, all_ref.at[2 * mine + core], local_sem.at[0])
    keep.start()
    for step in range(1, models):
        source = lax.rem(model + models - step, models)
        remote(
            vector_ref,
            model_ref.at[source],
            model_send.at[step - 1],
            model_recv.at[source],
            next_core,
        ).wait_recv()
    total = model_ref[0]
    for index in range(1, models):
        total = total + model_ref[index]
    group_ref[row] = total
    head_group[row] = head_ref[...]
    group_copies = []
    for step in range(1, groups):
        peer = (lax.rem(row + step, groups), model)
        for src, dst, send_sem, recv_sem in (
            (group_ref.at[row], group_ref.at[row], group_send, group_recv),
            (head_ref, head_group.at[row], head_send, head_recv),
        ):
            copy = remote(src, dst, send_sem.at[step - 1], recv_sem.at[row], peer)
            copy.start()
            group_copies.append(copy)
    far_slot = 2 * (1 - mine) + core
    along = []
    onward = []
    for piece in range(PIECES):
        across[piece].wait_recv()
        rows = part(half, piece)
        copy = remote(
            far_ref.at[rows, :],
            far_ref.at[rows, :],
            along_send.at[piece],
            along_recv.at[piece],
            next_row,
        )
        copy.start()
        along.append(copy)
        copy = remote(
            far_ref.at[rows, :],
            all_ref.at[far_slot, rows, :],
            onward_send.at[piece],
            onward_recv.at[piece],
            next_core,
        )
        copy.start()
        onward.append(copy)
    for piece in range(PIECES):
        along[piece].wait_recv()
        rows = part(1 - half, piece)
        copy = remote(
            far_ref.at[rows, :],
            all_ref.at[far_slot, rows, :],
            onward_send.at[PIECES + piece],
            onward_recv.at[PIECES + piece],
            next_core,
        )
        copy.start()
        onward.append(copy)
    keep_far = pltpu.make_async_copy(far_ref, all_ref.at[far_slot], local_sem.at[1])
    keep_far.start()
    for step in range(1, groups):
        source = lax.rem(row + groups - step, groups)
        for src, dst, send_sem, recv_sem in (
            (vector_ref, group_ref.at[source], group_send, group_recv),
            (head_ref, head_group.at[source], head_send, head_recv),
        ):
            remote(
                src, dst, send_sem.at[step - 1], recv_sem.at[source], next_row
            ).wait_recv()
    total = group_ref[0]
    head_total = head_group[0]
    for index in range(1, groups):
        total = total + group_ref[index]
        head_total = head_total + head_group[index]
    vector_out[...] = total
    head_out[...] = head_total
    for copy in across + along + model_copies + group_copies:
        copy.wait_send()
    beside.wait()
    for copy in onward:
        copy.wait()
    keep.wait()
    keep_far.wait()


def factor_exchange(factor, vector, head):
    groups, models = lax.axis_size("dp"), lax.axis_size("mp")
    dma = pltpu.SemaphoreType.DMA
    return pl.pallas_call(
        partial(factor_exchange_kernel, groups, models),
        out_shape=(
            jax.ShapeDtypeStruct((4, D, D), jnp.bfloat16),
            jax.ShapeDtypeStruct(vector.shape, jnp.float32),
            jax.ShapeDtypeStruct(head.shape, jnp.float32),
        ),
        in_specs=in_vmem(3),
        out_specs=tuple(in_vmem(3)),
        scratch_shapes=[
            pltpu.VMEM((D, D), jnp.bfloat16),
            pltpu.VMEM((models,) + vector.shape, jnp.float32),
            pltpu.VMEM((groups,) + vector.shape, jnp.float32),
            pltpu.VMEM((groups,) + head.shape, jnp.float32),
            dma((2,)),
            dma((1,)),
            dma((1,)),
            dma((PIECES,)),
            dma((PIECES,)),
            dma((PIECES,)),
            dma((PIECES,)),
            dma((2 * PIECES,)),
            dma((2 * PIECES,)),
            dma((models - 1,)),
            dma((models,)),
            dma((groups - 1,)),
            dma((groups,)),
            dma((groups - 1,)),
            dma((groups,)),
        ],
        compiler_params=pltpu.CompilerParams(
            collective_id=2, has_side_effects=True, vmem_limit_bytes=VMEM_BYTES
        ),
        name="factor_exchange",
    )(factor, vector, head)


def after(value, *earlier):
    return lax.optimization_barrier((value,) + earlier)[0]


SLICES = 4
TRANSFER_COST = pl.CostEstimate(
    flops=30_000_000_000, bytes_accessed=60_000_000, transcendentals=0
)


def model_peers(chips):
    row, chip, core = places()
    return [(row, chip * 2 + 1 - core)] + [
        (row, lax.rem(chip + step, chips) * 2 + core) for step in range(1, chips)
    ]


def model_gather_kernel(
    chips, own_ref, all_ref, keep_sem, beside_send, beside_recv, far_send, far_recv, onward_send, onward_recv
):
    _, chip, core = places()
    rows = own_ref.shape[0]
    size = rows // SLICES
    peers = model_peers(chips)
    greet(peers)

    def place(model, piece):
        return pl.ds(pl.multiple_of(model * rows + piece * size, size), size)

    here = chip * 2 + core
    far = {}
    for piece in range(SLICES):
        for step in range(1, chips):
            far[step, piece] = remote(
                own_ref.at[pl.ds(piece * size, size), :],
                all_ref.at[place(here, piece), :],
                far_send.at[step - 1, piece],
                far_recv.at[step - 1, piece],
                peers[step],
            )
            far[step, piece].start()
    whole = pl.ds(pl.multiple_of(here * rows, rows), rows)
    beside = remote(own_ref, all_ref.at[whole, :], beside_send.at[0], beside_recv.at[0], peers[0])
    beside.start()
    keep = pltpu.make_async_copy(own_ref, all_ref.at[whole, :], keep_sem.at[0])
    keep.start()
    onward = []
    for piece in range(SLICES):
        for step in range(1, chips):
            far[step, piece].wait_recv()
            source = lax.rem(chip + chips - step, chips) * 2 + core
            copy = remote(
                all_ref.at[place(source, piece), :],
                all_ref.at[place(source, piece), :],
                onward_send.at[step - 1, piece],
                onward_recv.at[step - 1, piece],
                peers[0],
            )
            copy.start()
            onward.append(copy)
    for copy in far.values():
        copy.wait_send()
    for copy in onward:
        copy.wait()
    beside.wait()
    keep.wait()


def model_gather(own, collective_id):
    models = lax.axis_size("mp")
    chips = models // 2
    dma = pltpu.SemaphoreType.DMA
    return pl.pallas_call(
        partial(model_gather_kernel, chips),
        out_shape=jax.ShapeDtypeStruct((models * own.shape[0], own.shape[1]), own.dtype),
        in_specs=in_vmem(1),
        out_specs=pl.BlockSpec(memory_space=pl.ANY),
        scratch_shapes=[dma((1,)), dma((1,)), dma((1,))] + [dma((chips - 1, SLICES))] * 4,
        compiler_params=pltpu.CompilerParams(
            collective_id=collective_id, has_side_effects=True, vmem_limit_bytes=VMEM_BYTES // 2
        ),
        cost_estimate=TRANSFER_COST,
        name="model_gather",
    )(own)


def model_scatter_kernel(
    chips, share_ref, sum_ref, core_ref, chip_ref, far_ref, core_send, core_recv, far_send, far_recv
):
    _, chip, core = places()
    rows = sum_ref.shape[0]
    size = rows // SLICES
    peers = model_peers(chips)
    greet(peers)

    def place(model, piece):
        return pl.ds(pl.multiple_of(model * rows + piece * size, size), size)

    beside = {}
    for step in list(range(1, chips)) + [0]:
        other = lax.rem(chip + step, chips)
        for piece in range(SLICES):
            inside = pl.ds(piece * size, size)
            beside[step, piece] = remote(
                share_ref.at[place(other * 2 + 1 - core, piece), :],
                core_ref.at[step, inside, :],
                core_send.at[step, piece],
                core_recv.at[step, piece],
                peers[0],
            )
            beside[step, piece].start()
    far = {}
    for step in range(1, chips):
        other = lax.rem(chip + step, chips)
        for piece in range(SLICES):
            inside = pl.ds(piece * size, size)
            beside[step, piece].wait()
            chip_ref[step - 1, inside, :] = (
                share_ref[place(other * 2 + core, piece), :].astype(jnp.float32)
                + core_ref[step, inside, :].astype(jnp.float32)
            ).astype(jnp.bfloat16)
            far[step, piece] = remote(
                chip_ref.at[step - 1, inside, :],
                far_ref.at[step - 1, inside, :],
                far_send.at[step - 1, piece],
                far_recv.at[step - 1, piece],
                peers[step],
            )
            far[step, piece].start()
    for piece in range(SLICES):
        inside = pl.ds(piece * size, size)
        beside[0, piece].wait()
        total = share_ref[place(chip * 2 + core, piece), :].astype(jnp.float32) + core_ref[
            0, inside, :
        ].astype(jnp.float32)
        for step in range(1, chips):
            far[step, piece].wait()
            total = total + far_ref[step - 1, inside, :].astype(jnp.float32)
        sum_ref[inside, :] = total


def model_scatter(share, collective_id):
    models = lax.axis_size("mp")
    chips = models // 2
    rows = share.shape[0] // models
    width = share.shape[1]
    dma = pltpu.SemaphoreType.DMA
    return pl.pallas_call(
        partial(model_scatter_kernel, chips),
        out_shape=jax.ShapeDtypeStruct((rows, width), jnp.float32),
        in_specs=in_vmem(1),
        out_specs=in_vmem(1)[0],
        scratch_shapes=[
            pltpu.VMEM((chips, rows, width), jnp.bfloat16),
            pltpu.VMEM((chips - 1, rows, width), jnp.bfloat16),
            pltpu.VMEM((chips - 1, rows, width), jnp.bfloat16),
            dma((chips, SLICES)),
            dma((chips, SLICES)),
            dma((chips - 1, SLICES)),
            dma((chips - 1, SLICES)),
        ],
        compiler_params=pltpu.CompilerParams(
            collective_id=collective_id, has_side_effects=True, vmem_limit_bytes=VMEM_BYTES // 2
        ),
        cost_estimate=TRANSFER_COST,
        name="model_scatter",
    )(share)


def sum_groups_kernel(groups, count, *refs):
    parts = refs[:count]
    sums = refs[count : 2 * count]
    one = refs[2 * count : 3 * count]
    mixed = refs[3 * count : 4 * count]
    two = refs[4 * count : 5 * count]
    (
        one_send,
        one_recv,
        two_send,
        two_recv,
        out_send,
        out_recv,
        back_send,
        back_recv,
    ) = refs[5 * count :]
    row = lax.axis_index("dp")
    model = lax.axis_index("mp")
    outer = groups // 2
    half = row % 2
    line = row // 2
    beside = (row + 1 - 2 * half, model)
    others = [(lax.rem(line + step, outer) * 2 + half, model) for step in range(1, outer)]
    greet([beside] + others)

    def place(ref, side, piece):
        size = ref.shape[0] // groups
        return pl.ds(pl.multiple_of(side * (ref.shape[0] // 2) + piece * size, size), size)

    steps = list(range(1, outer)) + [0]
    first = {}
    for step in steps:
        piece = lax.rem(line + step, outer)
        for index, ref in enumerate(parts):
            first[step, index] = remote(
                ref.at[place(ref, 1 - half, piece), :],
                one[index].at[step],
                one_send.at[step, index],
                one_recv.at[step, index],
                beside,
            )
            first[step, index].start()
    second = {}
    for step in range(1, outer):
        piece = lax.rem(line + step, outer)
        for index, ref in enumerate(parts):
            first[step, index].wait()
            mixed[index][step - 1] = (
                ref[place(ref, half, piece), :].astype(jnp.float32)
                + one[index][step].astype(jnp.float32)
            ).astype(jnp.bfloat16)
            second[step, index] = remote(
                mixed[index].at[step - 1],
                two[index].at[step - 1],
                two_send.at[step - 1, index],
                two_recv.at[step - 1, index],
                others[step - 1],
            )
            second[step, index].start()
    back = []
    third = {}
    for index, ref in enumerate(parts):
        here = place(ref, half, line)
        first[0, index].wait()
        total = ref[here, :].astype(jnp.float32) + one[index][0].astype(jnp.float32)
        for step in range(1, outer):
            second[step, index].wait()
            total = total + two[index][step - 1].astype(jnp.float32)
        sums[index][here, :] = total.astype(jnp.bfloat16)
        for step in range(1, outer):
            third[step, index] = remote(
                sums[index].at[here, :],
                sums[index].at[here, :],
                out_send.at[step - 1, index],
                out_recv.at[step - 1, index],
                others[step - 1],
            )
            third[step, index].start()
        copy = remote(
            sums[index].at[here, :],
            sums[index].at[here, :],
            back_send.at[0, index],
            back_recv.at[0, index],
            beside,
        )
        copy.start()
        back.append(copy)
    for step in range(1, outer):
        source = lax.rem(line + outer - step, outer)
        for index, ref in enumerate(parts):
            there = place(ref, half, source)
            remote(
                sums[index].at[there, :],
                sums[index].at[there, :],
                out_send.at[step - 1, index],
                out_recv.at[step - 1, index],
                others[step - 1],
            ).wait_recv()
            copy = remote(
                sums[index].at[there, :],
                sums[index].at[there, :],
                back_send.at[step, index],
                back_recv.at[step, index],
                beside,
            )
            copy.start()
            back.append(copy)
    for copy in third.values():
        copy.wait_send()
    for copy in back:
        copy.wait_send()
    for step in range(outer):
        source = lax.rem(line + outer - step, outer)
        for index, ref in enumerate(parts):
            there = place(ref, 1 - half, source)
            remote(
                sums[index].at[there, :],
                sums[index].at[there, :],
                back_send.at[step, index],
                back_recv.at[step, index],
                beside,
            ).wait_recv()


def sum_groups(parts, collective_id):
    groups = lax.axis_size("dp")
    outer = groups // 2
    if any(part.shape[0] % (16 * groups) for part in parts):
        return lax.psum(parts, "dp")
    dma = pltpu.SemaphoreType.DMA
    count = len(parts)

    def slots(number):
        return [
            pltpu.VMEM((number, part.shape[0] // groups, part.shape[1]), part.dtype)
            for part in parts
        ]

    return pl.pallas_call(
        partial(sum_groups_kernel, groups, count),
        out_shape=tuple(jax.ShapeDtypeStruct(part.shape, part.dtype) for part in parts),
        in_specs=in_vmem(count),
        out_specs=tuple(in_vmem(count)),
        scratch_shapes=slots(outer)
        + slots(outer - 1)
        + slots(outer - 1)
        + [dma((outer, count))] * 2
        + [dma((outer - 1, count))] * 4
        + [dma((outer, count))] * 2,
        compiler_params=pltpu.CompilerParams(
            collective_id=collective_id, has_side_effects=True, vmem_limit_bytes=VMEM_BYTES // 2
        ),
        cost_estimate=TRANSFER_COST,
        name="sum_groups",
    )(*parts)


QUERY = 256
KEY = 512
score_scale = HD ** (-0.5)
score_unit = score_scale / math.log(2.0)


def attend_kernel(low_ref, high_ref, first_ref, last_ref, q_ref, k_ref, v_ref, out_ref, lse_ref, top, total, acc):
    heads = q_ref.shape[0] // HD
    step = pl.program_id(0)
    top[...] = jnp.full(top.shape, neg_fill, jnp.float32)
    total[...] = jnp.zeros(total.shape, jnp.float32)
    acc[...] = jnp.zeros(acc.shape, jnp.float32)

    def key_block(index, carry):
        keys = pl.ds(pl.multiple_of(index * KEY, KEY), KEY)
        key_ids = lax.broadcasted_iota(jnp.int32, (KEY, QUERY), 0) + index * KEY
        allowed = (key_ids >= first_ref[...]) & (key_ids < last_ref[...])
        parts = [slice(head * HD, (head + 1) * HD) for head in range(heads)]
        scores = [
            jnp.where(allowed, tn_dot(k_ref[rows, keys], q_ref[rows, :]) * score_unit, neg_fill)
            for rows in parts
        ]
        old = [top[head : head + 1, :] for head in range(heads)]
        new = [
            jnp.maximum(old[head], jnp.max(scores[head], axis=0, keepdims=True))
            for head in range(heads)
        ]
        weights = [jnp.exp2(scores[head] - new[head]) for head in range(heads)]
        fade = [jnp.exp2(old[head] - new[head]) for head in range(heads)]
        added = [
            jnp.dot(
                v_ref[parts[head], keys],
                weights[head].astype(jnp.bfloat16),
                preferred_element_type=jnp.float32,
            )
            for head in range(heads)
        ]
        for head, rows in enumerate(parts):
            top[head : head + 1, :] = new[head]
            total[head : head + 1, :] = total[head : head + 1, :] * fade[head] + jnp.sum(
                weights[head], axis=0, keepdims=True
            )
            acc[rows, :] = acc[rows, :] * fade[head] + added[head]
        return carry

    lax.fori_loop(low_ref[step], high_ref[step], key_block, 0)
    for head in range(heads):
        rows = slice(head * HD, (head + 1) * HD)
        out_ref[rows, :] = (acc[rows, :] / total[head : head + 1, :]).astype(jnp.bfloat16)
        lse_ref[head : head + 1, :] = top[head : head + 1, :] + jnp.log2(total[head : head + 1, :])


def attend(mixed, spans):
    width = mixed.shape[0] // 3
    heads = width // HD
    low, high, first, last = spans
    return pl.pallas_call(
        attend_kernel,
        out_shape=(
            jax.ShapeDtypeStruct((width, ROWS_GRP), jnp.bfloat16),
            jax.ShapeDtypeStruct((heads, ROWS_GRP), jnp.float32),
        ),
        grid_spec=pltpu.PrefetchScalarGridSpec(
            num_scalar_prefetch=2,
            grid=(ROWS_GRP // QUERY,),
            in_specs=[
                pl.BlockSpec((1, QUERY), lambda i, *_: (0, i)),
                pl.BlockSpec((1, QUERY), lambda i, *_: (0, i)),
                pl.BlockSpec((width, QUERY), lambda i, *_: (0, i)),
                pl.BlockSpec((width, ROWS_GRP), lambda i, *_: (1, 0)),
                pl.BlockSpec((width, ROWS_GRP), lambda i, *_: (2, 0)),
            ],
            out_specs=[
                pl.BlockSpec((width, QUERY), lambda i, *_: (0, i)),
                pl.BlockSpec((heads, QUERY), lambda i, *_: (0, i)),
            ],
            scratch_shapes=[
                pltpu.VMEM((heads, QUERY), jnp.float32),
                pltpu.VMEM((heads, QUERY), jnp.float32),
                pltpu.VMEM((width, QUERY), jnp.float32),
            ],
        ),
        compiler_params=pltpu.CompilerParams(vmem_limit_bytes=VMEM_BYTES // 2),
        cost_estimate=pl.CostEstimate(
            flops=16 * heads * HD * ROWS_GRP * ROWS_GRP,
            bytes_accessed=8 * width * ROWS_GRP,
            transcendentals=0,
        ),
        name="attend",
    )(low, high, first, last, mixed, mixed, mixed)


def attend_back_kernel(
    low_ref, high_ref, first_ref, last_ref, q_ref, k_ref, v_ref, out_ref, grad_ref, lse_ref, mixed_ref, key_grad, value_grad, query_grad
):
    width = q_ref.shape[0]
    heads = width // HD
    step = pl.program_id(0)

    @pl.when(step == 0)
    def _():
        key_grad[...] = jnp.zeros(key_grad.shape, jnp.float32)
        value_grad[...] = jnp.zeros(value_grad.shape, jnp.float32)

    query_grad[...] = jnp.zeros(query_grad.shape, jnp.float32)
    inner = [
        jnp.sum(
            out_ref[head * HD : (head + 1) * HD, :].astype(jnp.float32)
            * grad_ref[head * HD : (head + 1) * HD, :].astype(jnp.float32),
            axis=0,
            keepdims=True,
        )
        for head in range(heads)
    ]

    def key_block(index, carry):
        keys = pl.ds(pl.multiple_of(index * KEY, KEY), KEY)
        key_ids = lax.broadcasted_iota(jnp.int32, (KEY, QUERY), 0) + index * KEY
        allowed = (key_ids >= first_ref[...]) & (key_ids < last_ref[...])
        for head in range(heads):
            rows = slice(head * HD, (head + 1) * HD)
            scores = tn_dot(k_ref[rows, keys], q_ref[rows, :]) * score_unit
            probs = jnp.exp2(jnp.where(allowed, scores, neg_fill) - lse_ref[head : head + 1, :])
            grad_probs = tn_dot(v_ref[rows, keys], grad_ref[rows, :])
            grad_scores = (probs * (grad_probs - inner[head])).astype(jnp.bfloat16)
            query_grad[rows, :] += jnp.dot(
                k_ref[rows, keys], grad_scores, preferred_element_type=jnp.float32
            )
            key_grad[rows, keys] += nt_dot(q_ref[rows, :], grad_scores)
            value_grad[rows, keys] += nt_dot(grad_ref[rows, :], probs.astype(jnp.bfloat16))
        return carry

    lax.fori_loop(low_ref[step], high_ref[step], key_block, 0)
    columns = pl.ds(pl.multiple_of(step * QUERY, QUERY), QUERY)
    mixed_ref[:width, columns] = (query_grad[...] * score_scale).astype(jnp.bfloat16)

    @pl.when(step == pl.num_programs(0) - 1)
    def _():
        mixed_ref[width : 2 * width, :] = (key_grad[...] * score_scale).astype(jnp.bfloat16)
        mixed_ref[2 * width :, :] = value_grad[...].astype(jnp.bfloat16)


def attend_back(mixed, attended, grad, lse, spans):
    width = mixed.shape[0] // 3
    heads = width // HD
    low, high, first, last = spans
    return pl.pallas_call(
        attend_back_kernel,
        out_shape=jax.ShapeDtypeStruct(mixed.shape, jnp.bfloat16),
        grid_spec=pltpu.PrefetchScalarGridSpec(
            num_scalar_prefetch=2,
            grid=(ROWS_GRP // QUERY,),
            in_specs=[
                pl.BlockSpec((1, QUERY), lambda i, *_: (0, i)),
                pl.BlockSpec((1, QUERY), lambda i, *_: (0, i)),
                pl.BlockSpec((width, QUERY), lambda i, *_: (0, i)),
                pl.BlockSpec((width, ROWS_GRP), lambda i, *_: (1, 0)),
                pl.BlockSpec((width, ROWS_GRP), lambda i, *_: (2, 0)),
                pl.BlockSpec((width, QUERY), lambda i, *_: (0, i)),
                pl.BlockSpec((width, QUERY), lambda i, *_: (0, i)),
                pl.BlockSpec((heads, QUERY), lambda i, *_: (0, i)),
            ],
            out_specs=pl.BlockSpec(mixed.shape, lambda i, *_: (0, 0)),
            scratch_shapes=[
                pltpu.VMEM((width, ROWS_GRP), jnp.float32),
                pltpu.VMEM((width, ROWS_GRP), jnp.float32),
                pltpu.VMEM((width, QUERY), jnp.float32),
            ],
        ),
        compiler_params=pltpu.CompilerParams(vmem_limit_bytes=VMEM_BYTES // 2),
        cost_estimate=pl.CostEstimate(
            flops=40 * heads * HD * ROWS_GRP * ROWS_GRP,
            bytes_accessed=20 * width * ROWS_GRP,
            transcendentals=0,
        ),
        name="attend_back",
    )(low, high, first, last, mixed, mixed, mixed, attended, grad, lse)


def on_device(
    patches,
    cotangent,
    item_group,
    item_length,
    project_in,
    project_out,
    expand_weight,
    shrink_weight,
    moment_in,
    moment_out,
    moment_expand,
    moment_shrink,
    norm_gains,
    shift_rows,
    head_shift,
    expand_shift,
    moment_gains,
    moment_shifts,
    moment_head,
    moment_expand_shift,
):
    dp_count = lax.axis_size("dp")
    group_index = lax.axis_index("dp")
    model_index = lax.axis_index("mp")
    own_rows = patches.shape[0]
    local_width = project_out.shape[0]
    local_hidden = shrink_weight.shape[0]
    used, first, last = group_spans(item_group, item_length, group_index)
    spans = (
        first[::QUERY] // KEY,
        (last[QUERY - 1 :: QUERY] + KEY - 1) // KEY,
        first[None, :],
        last[None, :],
    )
    own_ids = model_index * own_rows + jnp.arange(own_rows, dtype=jnp.int32)
    live_rows = (own_ids < used)[:, None]
    patch_values = patches.astype(jnp.float32)
    normed, norm_one_back = jax.vjp(layer_norm, patch_values, norm_gains[0], shift_rows[0])
    normed_all = model_gather(normed.astype(jnp.bfloat16), 3)
    in_low = project_in.astype(jnp.bfloat16).reshape(D, 3 * local_width)
    mixed_shift = jnp.concatenate(
        [head_shift[0], jnp.zeros((local_width,), jnp.float32), head_shift[1]]
    )
    mixed_low = (
        jnp.einsum("rd,dc->cr", normed_all, in_low, preferred_element_type=jnp.float32)
        + mixed_shift[:, None]
    ).astype(jnp.bfloat16)
    attended_low, log_totals = attend(mixed_low, spans)
    out_low = project_out.astype(jnp.bfloat16)
    attn_part = model_scatter(
        jnp.einsum(
            "cr,cd->rd", attended_low, out_low, preferred_element_type=jnp.float32
        ).astype(jnp.bfloat16),
        4,
    )
    middle = patch_values + attn_part + shift_rows[2]
    normed_two, norm_two_back = jax.vjp(layer_norm, middle, norm_gains[1], shift_rows[1])
    normed_low = normed_two.astype(jnp.bfloat16)
    gelu_exact = partial(jax.nn.gelu, approximate=False)
    out_grad = jnp.where(live_rows, cotangent, jnp.zeros_like(cotangent))
    out_grad_all = lax.all_gather(after(out_grad, normed_all), "mp", axis=0, tiled=True)
    normed_low, out_grad_all = lax.optimization_barrier((normed_low, out_grad_all))
    normed_two_all = model_gather(normed_low, 5)
    expand_low = expand_weight.astype(jnp.bfloat16)
    shrink_low = shrink_weight.astype(jnp.bfloat16)
    shift_part = lax.dynamic_slice_in_dim(expand_shift, model_index * local_hidden, local_hidden, 0)
    before = jnp.dot(normed_two_all, expand_low, preferred_element_type=jnp.float32) + shift_part
    hidden, gelu_back = jax.vjp(gelu_exact, before)
    hidden_low = hidden.astype(jnp.bfloat16)
    grad_shrink = jnp.einsum(
        "rf,rd->fd", hidden_low, out_grad_all, preferred_element_type=jnp.float32
    ).astype(jnp.bfloat16)
    grad_shrink, out_grad_all = lax.optimization_barrier((grad_shrink, out_grad_all))
    grad_hidden = jnp.einsum(
        "rd,fd->rf", out_grad_all, shrink_low, preferred_element_type=jnp.float32
    )
    grad_before = gelu_back(grad_hidden)[0].astype(jnp.bfloat16)
    grad_expand = jnp.einsum(
        "rd,rf->df", normed_two_all, grad_before, preferred_element_type=jnp.float32
    ).astype(jnp.bfloat16)
    grad_expand, grad_before = lax.optimization_barrier((grad_expand, grad_before))
    summed_expand, summed_shrink = lax.psum((grad_expand, grad_shrink), "dp")
    summed_expand = summed_expand.astype(jnp.float32)
    summed_shrink = summed_shrink.astype(jnp.float32)
    shift_sum = jnp.sum(grad_before, axis=0, dtype=jnp.float32)
    grad_expand_shift = lax.dynamic_update_slice_in_dim(
        jnp.zeros((FF,), jnp.float32), shift_sum, model_index * local_hidden, 0
    )
    two_share = jnp.einsum(
        "rf,df->rd", grad_before, expand_low, preferred_element_type=jnp.float32
    ).astype(jnp.bfloat16)
    grad_normed_two = model_scatter(two_share, 6)
    grad_middle_norm, gain_two_grad, shift_two_grad = norm_two_back(grad_normed_two)
    out_grad_values = out_grad.astype(jnp.float32)
    grad_middle = out_grad_values + grad_middle_norm
    middle_all = model_gather(grad_middle.astype(jnp.bfloat16), 7)
    grad_out = jnp.einsum("cr,rd->cd", attended_low, middle_all, preferred_element_type=jnp.float32)
    grad_attended = jnp.einsum(
        "cd,rd->cr", out_low, middle_all, preferred_element_type=jnp.float32
    ).astype(jnp.bfloat16)
    grad_mixed = attend_back(mixed_low, attended_low, grad_attended, log_totals, spans)
    grad_in = jnp.einsum("rd,cr->dc", normed_all, grad_mixed, preferred_element_type=jnp.float32)
    mixed_sums = jnp.sum(grad_mixed, axis=1, dtype=jnp.float32)
    grad_head = jnp.stack([mixed_sums[:local_width], mixed_sums[2 * local_width :]])
    one_share = jnp.einsum(
        "cr,dc->rd", grad_mixed, in_low, preferred_element_type=jnp.float32
    ).astype(jnp.bfloat16)
    ffn_share = jnp.dot(after(hidden_low, one_share), shrink_low, preferred_element_type=jnp.float32).astype(
        jnp.bfloat16
    )
    summed_out, summed_in = sum_groups(
        (grad_out.astype(jnp.bfloat16), grad_in.astype(jnp.bfloat16)), 8
    )
    summed_in = summed_in.astype(jnp.float32)
    summed_out = summed_out.astype(jnp.float32)
    grad_normed_one = lax.psum_scatter(
        one_share, "mp", scatter_dimension=0, tiled=True
    ).astype(jnp.float32)
    grad_patch_norm, gain_one_grad, shift_one_grad = norm_one_back(grad_normed_one)
    patch_grad = (grad_middle + grad_patch_norm).astype(jnp.bfloat16)
    gain_grads = jnp.stack([gain_one_grad, gain_two_grad])
    shift_grads = jnp.stack(
        [
            shift_one_grad,
            shift_two_grad,
            jnp.sum(grad_middle, axis=0),
            jnp.sum(out_grad_values, axis=0),
        ]
    )
    next_moment_in = muon_decay * moment_in + summed_in.reshape(D, 3, local_width)
    next_moment_out = muon_decay * moment_out + summed_out
    next_moment_expand = muon_decay * moment_expand + summed_expand
    next_moment_shrink = muon_decay * moment_shrink + summed_shrink
    matrices = [
        next_moment_in.reshape(D, 3 * local_width),
        next_moment_out,
        next_moment_expand,
        next_moment_shrink,
    ]
    orient = [True, False, True, False]
    lows = [matrix.astype(jnp.bfloat16) for matrix in matrices]
    own_gram = gram_exchange(gram_strips(*lows))
    ffn_part = lax.psum_scatter(
        ffn_share, "mp", scatter_dimension=0, tiled=True
    ).astype(jnp.float32)
    block_value = middle + ffn_part + shift_rows[3]
    block_out = jnp.where(live_rows, block_value, 0.0).astype(jnp.bfloat16)
    vector = jnp.concatenate(
        [gain_grads.reshape(-1), shift_grads.reshape(-1), grad_expand_shift]
    ).reshape(-1, 128)
    factors, vector_total, head_total = factor_exchange(
        sweep_chain(own_gram), vector, grad_head.reshape(-1, 128)
    )
    vector_total = vector_total.reshape(-1)
    gain_total = vector_total[: 2 * D].reshape(2, D)
    shift_total = vector_total[2 * D : 6 * D].reshape(4, D)
    expand_shift_total = vector_total[6 * D :]
    summed_head = head_total.reshape(2, local_width)
    scaled = [
        jnp.dot(factors[index], lows[index], preferred_element_type=jnp.float32)
        if orient[index]
        else jnp.einsum("rc,dc->rd", lows[index], factors[index], preferred_element_type=jnp.float32)
        for index in range(4)
    ]
    next_in = project_in - 1.25 * scaled[0].reshape(D, 3, local_width)
    next_out = project_out - 2.0 * scaled[1]
    next_expand = expand_weight - 1.0 * scaled[2]
    next_shrink = shrink_weight - 0.5 * scaled[3]
    vector_rate = 0.2 / math.sqrt(ROWS_GRP * dp_count)
    next_moment_gains = plain_decay * moment_gains + gain_total
    next_moment_shifts = plain_decay * moment_shifts + shift_total
    next_moment_head = plain_decay * moment_head + summed_head
    next_moment_expand_shift = plain_decay * moment_expand_shift + expand_shift_total
    next_gains = norm_gains - vector_rate * next_moment_gains
    next_shifts = shift_rows - vector_rate * next_moment_shifts
    next_head_shift = head_shift - vector_rate * next_moment_head
    next_expand_shift = expand_shift - vector_rate * next_moment_expand_shift
    return (
        block_out,
        patch_grad,
        next_in,
        next_out,
        next_expand,
        next_shrink,
        next_in.astype(jnp.bfloat16),
        next_out.astype(jnp.bfloat16),
        next_expand.astype(jnp.bfloat16),
        next_shrink.astype(jnp.bfloat16),
        next_moment_in,
        next_moment_out,
        next_moment_expand,
        next_moment_shrink,
        next_gains,
        next_shifts,
        next_head_shift,
        next_expand_shift,
        next_moment_gains,
        next_moment_shifts,
        next_moment_head,
        next_moment_expand_shift,
    )


def solution(mesh):
    placed = (
        P(("dp", "mp"), None),
        P(("dp", "mp"), None),
        P(),
        P(),
        P(None, None, "mp"),
        P("mp", None),
        P(None, "mp"),
        P("mp", None),
        P(None, None, "mp"),
        P("mp", None),
        P(None, "mp"),
        P("mp", None),
        P(),
        P(),
        P(None, "mp"),
        P(),
        P(),
        P(),
        P(None, "mp"),
        P(),
    )
    return jax.shard_map(
        on_device,
        mesh=mesh,
        in_specs=placed,
        out_specs=(
            P(("dp", "mp"), None),
            P(("dp", "mp"), None),
            P(None, None, "mp"),
            P("mp", None),
            P(None, "mp"),
            P("mp", None),
            P(None, None, "mp"),
            P("mp", None),
            P(None, "mp"),
            P("mp", None),
            P(None, None, "mp"),
            P("mp", None),
            P(None, "mp"),
            P("mp", None),
            P(),
            P(),
            P(None, "mp"),
            P(),
            P(),
            P(),
            P(None, "mp"),
            P(),
        ),
        check_vma=False,
    )
```

```python
from functools import partial
import math

import jax
import jax.numpy as jnp
from jax import lax
from jax.experimental import pallas as pl
from jax.experimental.pallas import tpu as pltpu
from jax.sharding import PartitionSpec as P


D = 1024
HD = 64
FF = 4096
ROWS_GRP = 2048
NS_ITERS = 5


norm_eps = 1e-06
coef_a = 3.4445
coef_b = -4.775
coef_c = 2.0315
muon_decay = 0.95
plain_decay = 0.5
neg_fill = -1e30


def layer_norm(values, scale_row, shift_row):
    row_mean = jnp.mean(values, axis=-1, keepdims=True)
    centered = values - row_mean
    spread = jnp.mean(centered * centered, axis=-1, keepdims=True)
    return centered * lax.rsqrt(spread + norm_eps) * scale_row + shift_row


def group_spans(item_group, item_length, group_index):
    member = item_group == group_index
    lengths = jnp.where(member, item_length, 0)
    item_ends = jnp.cumsum(lengths)
    item_starts = item_ends - lengths
    row_ids = jnp.arange(ROWS_GRP, dtype=jnp.int32)[:, None]
    inside = (row_ids >= item_starts[None, :]) & (row_ids < item_ends[None, :]) & member[None, :]
    used = item_ends[-1]
    live = row_ids[:, 0] < used
    first = jnp.where(live, jnp.max(jnp.where(inside, item_starts[None, :], 0), axis=1), used)
    last = jnp.where(live, jnp.max(jnp.where(inside, item_ends[None, :], 0), axis=1), ROWS_GRP)
    return used, first.astype(jnp.int32), last.astype(jnp.int32)


MESH = pl.DeviceIdType.MESH
CUT = 256
STRIPS = D // CUT
PAIRS = [(i, j) for i in range(STRIPS) for j in range(i, STRIPS)]
COUNT = len(PAIRS)
HALF = COUNT // 2
BLOCK = 512
VMEM_BYTES = 64 * 1024 * 1024 - 65536


def in_vmem(count):
    return [pl.BlockSpec(memory_space=pltpu.VMEM)] * count


def nt_dot(left, right):
    return lax.dot_general(
        left, right, (((1,), (1,)), ((), ())), preferred_element_type=jnp.float32
    )


def tn_dot(left, right):
    return lax.dot_general(
        left, right, (((0,), (0,)), ((), ())), preferred_element_type=jnp.float32
    )


def gram_kernel(in_ref, out_ref, expand_ref, shrink_ref, gram_ref):
    for slot, ref, by_columns in (
        (0, in_ref, True),
        (1, out_ref, False),
        (2, expand_ref, True),
        (3, shrink_ref, False),
    ):
        for i in range(STRIPS):
            if by_columns:
                strip = nt_dot(ref[i * CUT : (i + 1) * CUT, :], ref[i * CUT :, :])
            else:
                strip = tn_dot(ref[:, i * CUT : (i + 1) * CUT], ref[:, i * CUT :])
            for j in range(i, STRIPS):
                gram_ref[slot, PAIRS.index((i, j))] = strip[:, (j - i) * CUT : (j - i + 1) * CUT]


def gram_strips(low_in, low_out, low_expand, low_shrink):
    return pl.pallas_call(
        gram_kernel,
        out_shape=jax.ShapeDtypeStruct((4, COUNT, CUT, CUT), jnp.float32),
        in_specs=in_vmem(4),
        out_specs=in_vmem(1)[0],
        compiler_params=pltpu.CompilerParams(vmem_limit_bytes=VMEM_BYTES),
        name="gram_strips",
    )(low_in, low_out, low_expand, low_shrink)


def places():
    model = lax.axis_index("mp")
    return lax.axis_index("dp"), model // 2, model % 2


def greet(peers):
    barrier = pltpu.get_barrier_semaphore()
    for peer in peers:
        pl.semaphore_signal(barrier, inc=1, device_id=peer, device_id_type=MESH)
    pl.semaphore_wait(barrier, len(peers))


def remote(src, dst, send_sem, recv_sem, peer):
    return pltpu.make_async_remote_copy(
        src_ref=src,
        dst_ref=dst,
        send_sem=send_sem,
        recv_sem=recv_sem,
        device_id=peer,
        device_id_type=MESH,
    )


def gram_exchange_kernel(
    chips,
    gram_ref,
    own_ref,
    chip_ref,
    core_ref,
    far_ref,
    near_send,
    near_recv,
    core_send,
    core_recv,
    far_send,
    far_recv,
    row_send,
    row_recv,
):
    row, chip, core = places()
    mine = chip % 2
    theirs = 1 - mine
    half = row % 2
    beside = (row, chip * 2 + 1 - core)
    along = (row + 1 - 2 * half, chip * 2 + core)
    greet(
        [beside, along]
        + [(row, lax.rem(chip + step, chips) * 2 + core) for step in range(1, chips)]
    )
    near = [
        remote(
            gram_ref.at[2 * theirs + 1 - core, half * HALF + b],
            core_ref.at[theirs, half * HALF + b],
            near_send.at[b],
            near_recv.at[b],
            beside,
        )
        for b in range(HALF)
    ]
    kept = remote(
        gram_ref.at[2 * mine + 1 - core], core_ref.at[mine], core_send.at[0], core_recv.at[0], beside
    )
    for copy in near:
        copy.start()
    kept.start()
    far = {}

    def send_far(step, b):
        other = lax.rem(chip + step, chips)
        far[step, b] = remote(
            chip_ref.at[other % 2, half * HALF + b],
            far_ref.at[step - 1, half * HALF + b],
            far_send.at[step - 1, b],
            far_recv.at[step - 1, b],
            (row, other * 2 + core),
        )
        far[step, b].start()

    for b in range(HALF):
        near[b].wait()
        place = half * HALF + b
        chip_ref[theirs, place] = gram_ref[2 * theirs + core, place] + core_ref[theirs, place]
        for step in range(1, chips, 2):
            send_far(step, b)
    kept.wait()
    chip_ref[mine] = gram_ref[2 * mine + core] + core_ref[mine]
    for step in range(2, chips, 2):
        for b in range(HALF):
            send_far(step, b)
    onward = []
    for step in range(1, chips):
        for b in range(HALF):
            far[step, b].wait_recv()
            copy = remote(
                far_ref.at[step - 1, half * HALF + b],
                far_ref.at[step - 1, half * HALF + b],
                row_send.at[step - 1, b],
                row_recv.at[step - 1, b],
                along,
            )
            copy.start()
            onward.append(copy)
    for copy in far.values():
        copy.wait_send()
    for copy in onward:
        copy.wait()
    total = chip_ref[mine]
    for step in range(1, chips):
        total = total + far_ref[step - 1]
    own_ref[...] = total


def gram_exchange(grams):
    chips = lax.axis_size("mp") // 2
    shape = (COUNT, CUT, CUT)
    near = pltpu.SemaphoreType.DMA((HALF,))
    whole = pltpu.SemaphoreType.DMA((1,))
    away = pltpu.SemaphoreType.DMA((chips - 1, HALF))
    return pl.pallas_call(
        partial(gram_exchange_kernel, chips),
        out_shape=jax.ShapeDtypeStruct(shape, jnp.float32),
        in_specs=in_vmem(1),
        out_specs=in_vmem(1)[0],
        scratch_shapes=[
            pltpu.VMEM((2,) + shape, jnp.float32),
            pltpu.VMEM((2,) + shape, jnp.float32),
            pltpu.VMEM((chips - 1,) + shape, jnp.float32),
            near,
            near,
            whole,
            whole,
            away,
            away,
            away,
            away,
        ],
        compiler_params=pltpu.CompilerParams(
            collective_id=1, has_side_effects=True, vmem_limit_bytes=VMEM_BYTES
        ),
        name="gram_exchange",
    )(grams)


def chain_kernel(gram_ref, factor_ref, high, rest, inner, gram, first, first_low):
    rows_in = lax.broadcasted_iota(jnp.int32, (CUT, CUT), 0)
    diagonal = rows_in == lax.broadcasted_iota(jnp.int32, (CUT, CUT), 1)
    trace = jnp.zeros((), jnp.float32)
    for i in range(STRIPS):
        trace = trace + jnp.sum(jnp.where(diagonal, gram_ref[PAIRS.index((i, i))], 0.0))
    scale = 1.0 / (jnp.sqrt(jnp.full((8, 128), trace, jnp.float32)) + 1e-07)
    scale = jnp.max(scale)
    for index, (i, j) in enumerate(PAIRS):
        block = gram_ref[index] * scale * scale
        block_high = block.astype(jnp.bfloat16)
        block_rest = (block - block_high.astype(jnp.float32)).astype(jnp.bfloat16)
        high[i * CUT : (i + 1) * CUT, j * CUT : (j + 1) * CUT] = block_high
        rest[i * CUT : (i + 1) * CUT, j * CUT : (j + 1) * CUT] = block_rest
        if j > i:
            high[j * CUT : (j + 1) * CUT, i * CUT : (i + 1) * CUT] = block_high.T
            rest[j * CUT : (j + 1) * CUT, i * CUT : (i + 1) * CUT] = block_rest.T

    def rows_of(index):
        return pl.ds(pl.multiple_of(index * BLOCK, BLOCK), BLOCK)

    def product(left, right):
        return jnp.dot(left, right, preferred_element_type=jnp.float32)

    @pl.loop(0, D // BLOCK)
    def _(index):
        rows = rows_of(index)
        row_ids = lax.broadcasted_iota(jnp.int32, (BLOCK, D), 0) + index * BLOCK
        eye = (row_ids == lax.broadcasted_iota(jnp.int32, (BLOCK, D), 1)).astype(jnp.float32)
        second = product(high[rows, :], high[...])
        following = coef_a * eye + coef_b * high[rows, :].astype(jnp.float32) + coef_c * second
        factor_ref[rows, :] = following.astype(jnp.bfloat16)

    @pl.loop(1, NS_ITERS)
    def _(sweep):
        last = jnp.where(sweep == NS_ITERS - 1, scale, 1.0)

        @pl.loop(0, D // BLOCK)
        def _(index):
            rows = rows_of(index)
            inner[rows, :] = (
                nt_dot(high[rows, :], factor_ref[...]) + nt_dot(rest[rows, :], factor_ref[...])
            ).astype(jnp.bfloat16)

        @pl.loop(0, D // BLOCK)
        def _(index):
            rows = rows_of(index)
            block = product(factor_ref[rows, :], inner[...]).astype(jnp.bfloat16)
            gram[rows, :] = block
            term = product(block, factor_ref[...])
            first[rows, :] = term
            first_low[rows, :] = term.astype(jnp.bfloat16)

        @pl.loop(0, D // BLOCK)
        def _(index):
            rows = rows_of(index)
            second = product(gram[rows, :], first_low[...])
            following = (
                coef_a * factor_ref[rows, :].astype(jnp.float32)
                + coef_b * first[rows, :]
                + coef_c * second
            )
            factor_ref[rows, :] = (following * last).astype(jnp.bfloat16)


def sweep_chain(own_gram):
    low = pltpu.VMEM((D, D), jnp.bfloat16)
    return pl.pallas_call(
        chain_kernel,
        out_shape=jax.ShapeDtypeStruct((D, D), jnp.bfloat16),
        in_specs=in_vmem(1),
        out_specs=in_vmem(1)[0],
        scratch_shapes=[low, low, low, low, pltpu.VMEM((D, D), jnp.float32), low],
        compiler_params=pltpu.CompilerParams(vmem_limit_bytes=VMEM_BYTES),
        cost_estimate=pl.CostEstimate(
            flops=42 * D**3, bytes_accessed=6 * D * D, transcendentals=0
        ),
        name="sweep_chain",
    )(own_gram)


PIECES = 4
PIECE = D // 2 // PIECES


def factor_exchange_kernel(
    groups,
    models,
    own_ref,
    vector_ref,
    head_ref,
    all_ref,
    vector_out,
    head_out,
    far_ref,
    model_ref,
    group_ref,
    head_group,
    local_sem,
    beside_send,
    beside_recv,
    across_send,
    across_recv,
    along_send,
    along_recv,
    onward_send,
    onward_recv,
    model_send,
    model_recv,
    group_send,
    group_recv,
    head_send,
    head_recv,
):
    row, chip, core = places()
    model = chip * 2 + core
    mine = chip % 2
    half = row % 2
    next_core = (row, chip * 2 + 1 - core)
    next_chip = (row, (chip + 1 - 2 * mine) * 2 + core)
    next_row = (row + 1 - 2 * half, model)
    greet(
        [(row, lax.rem(model + step, models)) for step in range(1, models)]
        + [(lax.rem(row + step, groups), model) for step in range(1, groups)]
    )

    def part(which, piece):
        return pl.ds(pl.multiple_of(which * (D // 2) + piece * PIECE, PIECE), PIECE)

    model_ref[model] = vector_ref[...]
    model_copies = []
    for step in range(1, models):
        copy = remote(
            vector_ref,
            model_ref.at[model],
            model_send.at[step - 1],
            model_recv.at[model],
            (row, lax.rem(model + step, models)),
        )
        copy.start()
        model_copies.append(copy)
    across = []
    for piece in range(PIECES):
        rows = part(half, piece)
        copy = remote(
            own_ref.at[rows, :],
            far_ref.at[rows, :],
            across_send.at[piece],
            across_recv.at[piece],
            next_chip,
        )
        copy.start()
        across.append(copy)
    beside = remote(
        own_ref, all_ref.at[2 * mine + core], beside_send.at[0], beside_recv.at[0], next_core
    )
    beside.start()
    keep = pltpu.make_async_copy(own_ref, all_ref.at[2 * mine + core], local_sem.at[0])
    keep.start()
    for step in range(1, models):
        source = lax.rem(model + models - step, models)
        remote(
            vector_ref,
            model_ref.at[source],
            model_send.at[step - 1],
            model_recv.at[source],
            next_core,
        ).wait_recv()
    total = model_ref[0]
    for index in range(1, models):
        total = total + model_ref[index]
    group_ref[row] = total
    head_group[row] = head_ref[...]
    group_copies = []
    for step in range(1, groups):
        peer = (lax.rem(row + step, groups), model)
        for src, dst, send_sem, recv_sem in (
            (group_ref.at[row], group_ref.at[row], group_send, group_recv),
            (head_ref, head_group.at[row], head_send, head_recv),
        ):
            copy = remote(src, dst, send_sem.at[step - 1], recv_sem.at[row], peer)
            copy.start()
            group_copies.append(copy)
    far_slot = 2 * (1 - mine) + core
    along = []
    onward = []
    for piece in range(PIECES):
        across[piece].wait_recv()
        rows = part(half, piece)
        copy = remote(
            far_ref.at[rows, :],
            far_ref.at[rows, :],
            along_send.at[piece],
            along_recv.at[piece],
            next_row,
        )
        copy.start()
        along.append(copy)
        copy = remote(
            far_ref.at[rows, :],
            all_ref.at[far_slot, rows, :],
            onward_send.at[piece],
            onward_recv.at[piece],
            next_core,
        )
        copy.start()
        onward.append(copy)
    for piece in range(PIECES):
        along[piece].wait_recv()
        rows = part(1 - half, piece)
        copy = remote(
            far_ref.at[rows, :],
            all_ref.at[far_slot, rows, :],
            onward_send.at[PIECES + piece],
            onward_recv.at[PIECES + piece],
            next_core,
        )
        copy.start()
        onward.append(copy)
    keep_far = pltpu.make_async_copy(far_ref, all_ref.at[far_slot], local_sem.at[1])
    keep_far.start()
    for step in range(1, groups):
        source = lax.rem(row + groups - step, groups)
        for src, dst, send_sem, recv_sem in (
            (vector_ref, group_ref.at[source], group_send, group_recv),
            (head_ref, head_group.at[source], head_send, head_recv),
        ):
            remote(
                src, dst, send_sem.at[step - 1], recv_sem.at[source], next_row
            ).wait_recv()
    total = group_ref[0]
    head_total = head_group[0]
    for index in range(1, groups):
        total = total + group_ref[index]
        head_total = head_total + head_group[index]
    vector_out[...] = total
    head_out[...] = head_total
    for copy in across + along + model_copies + group_copies:
        copy.wait_send()
    beside.wait()
    for copy in onward:
        copy.wait()
    keep.wait()
    keep_far.wait()


def factor_exchange(factor, vector, head):
    groups, models = lax.axis_size("dp"), lax.axis_size("mp")
    dma = pltpu.SemaphoreType.DMA
    return pl.pallas_call(
        partial(factor_exchange_kernel, groups, models),
        out_shape=(
            jax.ShapeDtypeStruct((4, D, D), jnp.bfloat16),
            jax.ShapeDtypeStruct(vector.shape, jnp.float32),
            jax.ShapeDtypeStruct(head.shape, jnp.float32),
        ),
        in_specs=in_vmem(3),
        out_specs=tuple(in_vmem(3)),
        scratch_shapes=[
            pltpu.VMEM((D, D), jnp.bfloat16),
            pltpu.VMEM((models,) + vector.shape, jnp.float32),
            pltpu.VMEM((groups,) + vector.shape, jnp.float32),
            pltpu.VMEM((groups,) + head.shape, jnp.float32),
            dma((2,)),
            dma((1,)),
            dma((1,)),
            dma((PIECES,)),
            dma((PIECES,)),
            dma((PIECES,)),
            dma((PIECES,)),
            dma((2 * PIECES,)),
            dma((2 * PIECES,)),
            dma((models - 1,)),
            dma((models,)),
            dma((groups - 1,)),
            dma((groups,)),
            dma((groups - 1,)),
            dma((groups,)),
        ],
        compiler_params=pltpu.CompilerParams(
            collective_id=2, has_side_effects=True, vmem_limit_bytes=VMEM_BYTES
        ),
        name="factor_exchange",
    )(factor, vector, head)


def after(value, *earlier):
    return lax.optimization_barrier((value,) + earlier)[0]


SLICES = 4
TRANSFER_COST = pl.CostEstimate(
    flops=30_000_000_000, bytes_accessed=60_000_000, transcendentals=0
)


def model_peers(chips):
    row, chip, core = places()
    return [(row, chip * 2 + 1 - core)] + [
        (row, lax.rem(chip + step, chips) * 2 + core) for step in range(1, chips)
    ]


def model_gather_kernel(
    chips, own_ref, all_ref, keep_sem, beside_send, beside_recv, far_send, far_recv, onward_send, onward_recv
):
    _, chip, core = places()
    rows = own_ref.shape[0]
    size = rows // SLICES
    peers = model_peers(chips)
    greet(peers)

    def place(model, piece):
        return pl.ds(pl.multiple_of(model * rows + piece * size, size), size)

    here = chip * 2 + core
    far = {}
    for piece in range(SLICES):
        for step in range(1, chips):
            far[step, piece] = remote(
                own_ref.at[pl.ds(piece * size, size), :],
                all_ref.at[place(here, piece), :],
                far_send.at[step - 1, piece],
                far_recv.at[step - 1, piece],
                peers[step],
            )
            far[step, piece].start()
    whole = pl.ds(pl.multiple_of(here * rows, rows), rows)
    beside = remote(own_ref, all_ref.at[whole, :], beside_send.at[0], beside_recv.at[0], peers[0])
    beside.start()
    keep = pltpu.make_async_copy(own_ref, all_ref.at[whole, :], keep_sem.at[0])
    keep.start()
    onward = []
    for piece in range(SLICES):
        for step in range(1, chips):
            far[step, piece].wait_recv()
            source = lax.rem(chip + chips - step, chips) * 2 + core
            copy = remote(
                all_ref.at[place(source, piece), :],
                all_ref.at[place(source, piece), :],
                onward_send.at[step - 1, piece],
                onward_recv.at[step - 1, piece],
                peers[0],
            )
            copy.start()
            onward.append(copy)
    for copy in far.values():
        copy.wait_send()
    for copy in onward:
        copy.wait()
    beside.wait()
    keep.wait()


def model_gather(own, collective_id):
    models = lax.axis_size("mp")
    chips = models // 2
    dma = pltpu.SemaphoreType.DMA
    return pl.pallas_call(
        partial(model_gather_kernel, chips),
        out_shape=jax.ShapeDtypeStruct((models * own.shape[0], own.shape[1]), own.dtype),
        in_specs=in_vmem(1),
        out_specs=pl.BlockSpec(memory_space=pl.ANY),
        scratch_shapes=[dma((1,)), dma((1,)), dma((1,))] + [dma((chips - 1, SLICES))] * 4,
        compiler_params=pltpu.CompilerParams(
            collective_id=collective_id, has_side_effects=True, vmem_limit_bytes=VMEM_BYTES // 2
        ),
        cost_estimate=TRANSFER_COST,
        name="model_gather",
    )(own)


def model_scatter_kernel(
    chips, share_ref, sum_ref, core_ref, chip_ref, far_ref, core_send, core_recv, far_send, far_recv
):
    _, chip, core = places()
    rows = sum_ref.shape[0]
    size = rows // SLICES
    peers = model_peers(chips)
    greet(peers)

    def place(model, piece):
        return pl.ds(pl.multiple_of(model * rows + piece * size, size), size)

    beside = {}
    for step in list(range(1, chips)) + [0]:
        other = lax.rem(chip + step, chips)
        for piece in range(SLICES):
            inside = pl.ds(piece * size, size)
            beside[step, piece] = remote(
                share_ref.at[place(other * 2 + 1 - core, piece), :],
                core_ref.at[step, inside, :],
                core_send.at[step, piece],
                core_recv.at[step, piece],
                peers[0],
            )
            beside[step, piece].start()
    far = {}
    for step in range(1, chips):
        other = lax.rem(chip + step, chips)
        for piece in range(SLICES):
            inside = pl.ds(piece * size, size)
            beside[step, piece].wait()
            chip_ref[step - 1, inside, :] = (
                share_ref[place(other * 2 + core, piece), :].astype(jnp.float32)
                + core_ref[step, inside, :].astype(jnp.float32)
            ).astype(jnp.bfloat16)
            far[step, piece] = remote(
                chip_ref.at[step - 1, inside, :],
                far_ref.at[step - 1, inside, :],
                far_send.at[step - 1, piece],
                far_recv.at[step - 1, piece],
                peers[step],
            )
            far[step, piece].start()
    for piece in range(SLICES):
        inside = pl.ds(piece * size, size)
        beside[0, piece].wait()
        total = share_ref[place(chip * 2 + core, piece), :].astype(jnp.float32) + core_ref[
            0, inside, :
        ].astype(jnp.float32)
        for step in range(1, chips):
            far[step, piece].wait()
            total = total + far_ref[step - 1, inside, :].astype(jnp.float32)
        sum_ref[inside, :] = total


def model_scatter(share, collective_id):
    models = lax.axis_size("mp")
    chips = models // 2
    rows = share.shape[0] // models
    width = share.shape[1]
    dma = pltpu.SemaphoreType.DMA
    return pl.pallas_call(
        partial(model_scatter_kernel, chips),
        out_shape=jax.ShapeDtypeStruct((rows, width), jnp.float32),
        in_specs=in_vmem(1),
        out_specs=in_vmem(1)[0],
        scratch_shapes=[
            pltpu.VMEM((chips, rows, width), jnp.bfloat16),
            pltpu.VMEM((chips - 1, rows, width), jnp.bfloat16),
            pltpu.VMEM((chips - 1, rows, width), jnp.bfloat16),
            dma((chips, SLICES)),
            dma((chips, SLICES)),
            dma((chips - 1, SLICES)),
            dma((chips - 1, SLICES)),
        ],
        compiler_params=pltpu.CompilerParams(
            collective_id=collective_id, has_side_effects=True, vmem_limit_bytes=VMEM_BYTES // 2
        ),
        cost_estimate=TRANSFER_COST,
        name="model_scatter",
    )(share)


def sum_groups_kernel(groups, count, *refs):
    parts = refs[:count]
    sums = refs[count : 2 * count]
    one = refs[2 * count : 3 * count]
    mixed = refs[3 * count : 4 * count]
    two = refs[4 * count : 5 * count]
    (
        one_send,
        one_recv,
        two_send,
        two_recv,
        out_send,
        out_recv,
        back_send,
        back_recv,
    ) = refs[5 * count :]
    row = lax.axis_index("dp")
    model = lax.axis_index("mp")
    outer = groups // 2
    half = row % 2
    line = row // 2
    beside = (row + 1 - 2 * half, model)
    others = [(lax.rem(line + step, outer) * 2 + half, model) for step in range(1, outer)]
    greet([beside] + others)

    def place(ref, side, piece):
        size = ref.shape[0] // groups
        return pl.ds(pl.multiple_of(side * (ref.shape[0] // 2) + piece * size, size), size)

    steps = list(range(1, outer)) + [0]
    first = {}
    for step in steps:
        piece = lax.rem(line + step, outer)
        for index, ref in enumerate(parts):
            first[step, index] = remote(
                ref.at[place(ref, 1 - half, piece), :],
                one[index].at[step],
                one_send.at[step, index],
                one_recv.at[step, index],
                beside,
            )
            first[step, index].start()
    second = {}
    for step in range(1, outer):
        piece = lax.rem(line + step, outer)
        for index, ref in enumerate(parts):
            first[step, index].wait()
            mixed[index][step - 1] = (
                ref[place(ref, half, piece), :].astype(jnp.float32)
                + one[index][step].astype(jnp.float32)
            ).astype(jnp.bfloat16)
            second[step, index] = remote(
                mixed[index].at[step - 1],
                two[index].at[step - 1],
                two_send.at[step - 1, index],
                two_recv.at[step - 1, index],
                others[step - 1],
            )
            second[step, index].start()
    back = []
    third = {}
    for index, ref in enumerate(parts):
        here = place(ref, half, line)
        first[0, index].wait()
        total = ref[here, :].astype(jnp.float32) + one[index][0].astype(jnp.float32)
        for step in range(1, outer):
            second[step, index].wait()
            total = total + two[index][step - 1].astype(jnp.float32)
        sums[index][here, :] = total.astype(jnp.bfloat16)
        for step in range(1, outer):
            third[step, index] = remote(
                sums[index].at[here, :],
                sums[index].at[here, :],
                out_send.at[step - 1, index],
                out_recv.at[step - 1, index],
                others[step - 1],
            )
            third[step, index].start()
        copy = remote(
            sums[index].at[here, :],
            sums[index].at[here, :],
            back_send.at[0, index],
            back_recv.at[0, index],
            beside,
        )
        copy.start()
        back.append(copy)
    for step in range(1, outer):
        source = lax.rem(line + outer - step, outer)
        for index, ref in enumerate(parts):
            there = place(ref, half, source)
            remote(
                sums[index].at[there, :],
                sums[index].at[there, :],
                out_send.at[step - 1, index],
                out_recv.at[step - 1, index],
                others[step - 1],
            ).wait_recv()
            copy = remote(
                sums[index].at[there, :],
                sums[index].at[there, :],
                back_send.at[step, index],
                back_recv.at[step, index],
                beside,
            )
            copy.start()
            back.append(copy)
    for copy in third.values():
        copy.wait_send()
    for copy in back:
        copy.wait_send()
    for step in range(outer):
        source = lax.rem(line + outer - step, outer)
        for index, ref in enumerate(parts):
            there = place(ref, 1 - half, source)
            remote(
                sums[index].at[there, :],
                sums[index].at[there, :],
                back_send.at[step, index],
                back_recv.at[step, index],
                beside,
            ).wait_recv()


def sum_groups(parts, collective_id):
    groups = lax.axis_size("dp")
    outer = groups // 2
    if any(part.shape[0] % (16 * groups) for part in parts):
        return lax.psum(parts, "dp")
    dma = pltpu.SemaphoreType.DMA
    count = len(parts)

    def slots(number):
        return [
            pltpu.VMEM((number, part.shape[0] // groups, part.shape[1]), part.dtype)
            for part in parts
        ]

    return pl.pallas_call(
        partial(sum_groups_kernel, groups, count),
        out_shape=tuple(jax.ShapeDtypeStruct(part.shape, part.dtype) for part in parts),
        in_specs=in_vmem(count),
        out_specs=tuple(in_vmem(count)),
        scratch_shapes=slots(outer)
        + slots(outer - 1)
        + slots(outer - 1)
        + [dma((outer, count))] * 2
        + [dma((outer - 1, count))] * 4
        + [dma((outer, count))] * 2,
        compiler_params=pltpu.CompilerParams(
            collective_id=collective_id, has_side_effects=True, vmem_limit_bytes=VMEM_BYTES // 2
        ),
        cost_estimate=TRANSFER_COST,
        name="sum_groups",
    )(*parts)


MLP_ROWS = 256


def mlp_kernel(x_ref, og_ref, we_ref, ws_ref, shift_ref, hidden_ref, before_ref, two_ref, ffn_ref, sum_ref):
    @pl.when(pl.program_id(0) == 0)
    def _():
        sum_ref[...] = jnp.zeros(sum_ref.shape, jnp.float32)

    before = jnp.dot(x_ref[...], we_ref[...], preferred_element_type=jnp.float32) + shift_ref[...]
    grad_hidden = nt_dot(og_ref[...], ws_ref[...])
    cover = 0.5 + 0.5 * lax.erf(before * math.sqrt(0.5))
    hidden = (before * cover).astype(jnp.bfloat16)
    hidden_ref[...] = hidden
    density = jnp.exp(-0.5 * before * before) * (1.0 / math.sqrt(2.0 * math.pi))
    grad_before = (grad_hidden * (cover + before * density)).astype(jnp.bfloat16)
    before_ref[...] = grad_before
    sum_ref[...] += jnp.sum(grad_before.astype(jnp.float32), axis=0, keepdims=True)
    ffn_ref[...] = jnp.dot(hidden, ws_ref[...], preferred_element_type=jnp.float32).astype(
        jnp.bfloat16
    )
    two_ref[...] = nt_dot(grad_before, we_ref[...]).astype(jnp.bfloat16)


def mlp(rows, out_grad, expand_low, shrink_low, shift):
    count, width = rows.shape
    inner = expand_low.shape[1]

    def block(columns):
        return pl.BlockSpec((MLP_ROWS, columns), lambda i: (i, 0))

    def fixed(shape):
        return pl.BlockSpec(shape, lambda i: (0, 0))

    low = jnp.bfloat16
    return pl.pallas_call(
        mlp_kernel,
        grid=(count // MLP_ROWS,),
        out_shape=(
            jax.ShapeDtypeStruct((count, inner), low),
            jax.ShapeDtypeStruct((count, inner), low),
            jax.ShapeDtypeStruct((count, width), low),
            jax.ShapeDtypeStruct((count, width), low),
            jax.ShapeDtypeStruct((1, inner), jnp.float32),
        ),
        in_specs=[
            block(width),
            block(width),
            fixed((width, inner)),
            fixed((inner, width)),
            fixed((1, inner)),
        ],
        out_specs=(block(inner), block(inner), block(width), block(width), fixed((1, inner))),
        compiler_params=pltpu.CompilerParams(vmem_limit_bytes=VMEM_BYTES // 2),
        cost_estimate=pl.CostEstimate(
            flops=8 * count * inner * width, bytes_accessed=12 * count * width, transcendentals=0
        ),
        name="mlp",
    )(rows, out_grad, expand_low, shrink_low, shift.reshape(1, inner))


QUERY = 256
KEY = 512
TOGETHER = 4
score_scale = HD ** (-0.5)
score_unit = score_scale / math.log(2.0)


def attend_kernel(low_ref, high_ref, first_ref, last_ref, q_ref, k_ref, v_ref, out_ref, lse_ref, top, total, acc):
    heads = q_ref.shape[0] // HD
    step = pl.program_id(0)
    top[...] = jnp.full(top.shape, neg_fill, jnp.float32)
    total[...] = jnp.zeros(total.shape, jnp.float32)
    acc[...] = jnp.zeros(acc.shape, jnp.float32)

    def key_block(index, carry):
        keys = pl.ds(pl.multiple_of(index * KEY, KEY), KEY)
        key_ids = lax.broadcasted_iota(jnp.int32, (KEY, QUERY), 0) + index * KEY
        allowed = (key_ids >= first_ref[...]) & (key_ids < last_ref[...])
        parts = [slice(head * HD, (head + 1) * HD) for head in range(heads)]
        scores = [
            jnp.where(allowed, tn_dot(k_ref[rows, keys], q_ref[rows, :]) * score_unit, neg_fill)
            for rows in parts
        ]
        old = [top[head : head + 1, :] for head in range(heads)]
        new = [
            jnp.maximum(old[head], jnp.max(scores[head], axis=0, keepdims=True))
            for head in range(heads)
        ]
        weights = [jnp.exp2(scores[head] - new[head]) for head in range(heads)]
        fade = [jnp.exp2(old[head] - new[head]) for head in range(heads)]
        added = [
            jnp.dot(
                v_ref[parts[head], keys],
                weights[head].astype(jnp.bfloat16),
                preferred_element_type=jnp.float32,
            )
            for head in range(heads)
        ]
        for head, rows in enumerate(parts):
            top[head : head + 1, :] = new[head]
            total[head : head + 1, :] = total[head : head + 1, :] * fade[head] + jnp.sum(
                weights[head], axis=0, keepdims=True
            )
            acc[rows, :] = acc[rows, :] * fade[head] + added[head]
        return carry

    lax.fori_loop(low_ref[step], high_ref[step], key_block, 0)
    for head in range(heads):
        rows = slice(head * HD, (head + 1) * HD)
        out_ref[rows, :] = (acc[rows, :] / total[head : head + 1, :]).astype(jnp.bfloat16)
        lse_ref[head : head + 1, :] = top[head : head + 1, :] + jnp.log2(total[head : head + 1, :])


def attend(mixed, spans):
    width = mixed.shape[0] // 3
    heads = width // HD
    low, high, first, last = spans
    return pl.pallas_call(
        attend_kernel,
        out_shape=(
            jax.ShapeDtypeStruct((width, ROWS_GRP), jnp.bfloat16),
            jax.ShapeDtypeStruct((heads, ROWS_GRP), jnp.float32),
        ),
        grid_spec=pltpu.PrefetchScalarGridSpec(
            num_scalar_prefetch=2,
            grid=(ROWS_GRP // QUERY,),
            in_specs=[
                pl.BlockSpec((1, QUERY), lambda i, *_: (0, i)),
                pl.BlockSpec((1, QUERY), lambda i, *_: (0, i)),
                pl.BlockSpec((width, QUERY), lambda i, *_: (0, i)),
                pl.BlockSpec((width, ROWS_GRP), lambda i, *_: (1, 0)),
                pl.BlockSpec((width, ROWS_GRP), lambda i, *_: (2, 0)),
            ],
            out_specs=[
                pl.BlockSpec((width, QUERY), lambda i, *_: (0, i)),
                pl.BlockSpec((heads, QUERY), lambda i, *_: (0, i)),
            ],
            scratch_shapes=[
                pltpu.VMEM((heads, QUERY), jnp.float32),
                pltpu.VMEM((heads, QUERY), jnp.float32),
                pltpu.VMEM((width, QUERY), jnp.float32),
            ],
        ),
        compiler_params=pltpu.CompilerParams(vmem_limit_bytes=VMEM_BYTES // 2),
        cost_estimate=pl.CostEstimate(
            flops=16 * heads * HD * ROWS_GRP * ROWS_GRP,
            bytes_accessed=8 * width * ROWS_GRP,
            transcendentals=0,
        ),
        name="attend",
    )(low, high, first, last, mixed, mixed, mixed)


def attend_back_kernel(
    low_ref, high_ref, first_ref, last_ref, q_ref, k_ref, v_ref, out_ref, grad_ref, lse_ref, mixed_ref, sums_ref, key_grad, value_grad, query_grad
):
    width = q_ref.shape[0]
    heads = width // HD
    step = pl.program_id(0)

    @pl.when(step == 0)
    def _():
        key_grad[...] = jnp.zeros(key_grad.shape, jnp.float32)
        value_grad[...] = jnp.zeros(value_grad.shape, jnp.float32)
        sums_ref[...] = jnp.zeros(sums_ref.shape, jnp.float32)

    query_grad[...] = jnp.zeros(query_grad.shape, jnp.float32)
    inner = [
        jnp.sum(
            out_ref[head * HD : (head + 1) * HD, :].astype(jnp.float32)
            * grad_ref[head * HD : (head + 1) * HD, :].astype(jnp.float32),
            axis=0,
            keepdims=True,
        )
        for head in range(heads)
    ]

    def key_block(index, carry):
        keys = pl.ds(pl.multiple_of(index * KEY, KEY), KEY)
        key_ids = lax.broadcasted_iota(jnp.int32, (KEY, QUERY), 0) + index * KEY
        allowed = (key_ids >= first_ref[...]) & (key_ids < last_ref[...])
        parts = [slice(head * HD, (head + 1) * HD) for head in range(heads)]
        for pair in range(0, heads, TOGETHER):
            chosen = range(pair, min(pair + TOGETHER, heads))
            probs = {}
            grad_scores = {}
            for head in chosen:
                scores = tn_dot(k_ref[parts[head], keys], q_ref[parts[head], :]) * score_unit
                probs[head] = jnp.exp2(
                    jnp.where(allowed, scores, neg_fill) - lse_ref[head : head + 1, :]
                )
            for head in chosen:
                grad_probs = tn_dot(v_ref[parts[head], keys], grad_ref[parts[head], :])
                grad_scores[head] = (probs[head] * (grad_probs - inner[head])).astype(jnp.bfloat16)
            for head in chosen:
                rows = parts[head]
                query_grad[rows, :] += jnp.dot(
                    k_ref[rows, keys], grad_scores[head], preferred_element_type=jnp.float32
                )
                key_grad[rows, keys] += nt_dot(q_ref[rows, :], grad_scores[head])
                value_grad[rows, keys] += nt_dot(
                    grad_ref[rows, :], probs[head].astype(jnp.bfloat16)
                )
        return carry

    lax.fori_loop(low_ref[step], high_ref[step], key_block, 0)
    columns = pl.ds(pl.multiple_of(step * QUERY, QUERY), QUERY)
    query_low = (query_grad[...] * score_scale).astype(jnp.bfloat16)
    mixed_ref[:width, columns] = query_low
    sums_ref[:width, :] += jnp.sum(query_low.astype(jnp.float32), axis=1, keepdims=True)

    @pl.when(step == pl.num_programs(0) - 1)
    def _():
        mixed_ref[width : 2 * width, :] = (key_grad[...] * score_scale).astype(jnp.bfloat16)
        value_low = value_grad[...].astype(jnp.bfloat16)
        mixed_ref[2 * width :, :] = value_low
        sums_ref[width:, :] = jnp.sum(value_low.astype(jnp.float32), axis=1, keepdims=True)


def attend_back(mixed, attended, grad, lse, spans):
    width = mixed.shape[0] // 3
    heads = width // HD
    low, high, first, last = spans
    return pl.pallas_call(
        attend_back_kernel,
        out_shape=(
            jax.ShapeDtypeStruct(mixed.shape, jnp.bfloat16),
            jax.ShapeDtypeStruct((2 * width, 1), jnp.float32),
        ),
        grid_spec=pltpu.PrefetchScalarGridSpec(
            num_scalar_prefetch=2,
            grid=(ROWS_GRP // QUERY,),
            in_specs=[
                pl.BlockSpec((1, QUERY), lambda i, *_: (0, i)),
                pl.BlockSpec((1, QUERY), lambda i, *_: (0, i)),
                pl.BlockSpec((width, QUERY), lambda i, *_: (0, i)),
                pl.BlockSpec((width, ROWS_GRP), lambda i, *_: (1, 0)),
                pl.BlockSpec((width, ROWS_GRP), lambda i, *_: (2, 0)),
                pl.BlockSpec((width, QUERY), lambda i, *_: (0, i)),
                pl.BlockSpec((width, QUERY), lambda i, *_: (0, i)),
                pl.BlockSpec((heads, QUERY), lambda i, *_: (0, i)),
            ],
            out_specs=[
                pl.BlockSpec(mixed.shape, lambda i, *_: (0, 0)),
                pl.BlockSpec((2 * width, 1), lambda i, *_: (0, 0)),
            ],
            scratch_shapes=[
                pltpu.VMEM((width, ROWS_GRP), jnp.float32),
                pltpu.VMEM((width, ROWS_GRP), jnp.float32),
                pltpu.VMEM((width, QUERY), jnp.float32),
            ],
        ),
        compiler_params=pltpu.CompilerParams(vmem_limit_bytes=VMEM_BYTES // 2),
        cost_estimate=pl.CostEstimate(
            flops=40 * heads * HD * ROWS_GRP * ROWS_GRP,
            bytes_accessed=20 * width * ROWS_GRP,
            transcendentals=0,
        ),
        name="attend_back",
    )(low, high, first, last, mixed, mixed, mixed, attended, grad, lse)


def on_device(
    patches,
    cotangent,
    item_group,
    item_length,
    project_in,
    project_out,
    expand_weight,
    shrink_weight,
    moment_in,
    moment_out,
    moment_expand,
    moment_shrink,
    norm_gains,
    shift_rows,
    head_shift,
    expand_shift,
    moment_gains,
    moment_shifts,
    moment_head,
    moment_expand_shift,
):
    dp_count = lax.axis_size("dp")
    group_index = lax.axis_index("dp")
    model_index = lax.axis_index("mp")
    own_rows = patches.shape[0]
    local_width = project_out.shape[0]
    local_hidden = shrink_weight.shape[0]
    used, first, last = group_spans(item_group, item_length, group_index)
    spans = (
        first[::QUERY] // KEY,
        (last[QUERY - 1 :: QUERY] + KEY - 1) // KEY,
        first[None, :],
        last[None, :],
    )
    own_ids = model_index * own_rows + jnp.arange(own_rows, dtype=jnp.int32)
    live_rows = (own_ids < used)[:, None]
    patch_values = patches.astype(jnp.float32)
    normed, norm_one_back = jax.vjp(layer_norm, patch_values, norm_gains[0], shift_rows[0])
    normed_all = model_gather(normed.astype(jnp.bfloat16), 3)
    in_low = project_in.astype(jnp.bfloat16).reshape(D, 3 * local_width)
    mixed_shift = jnp.concatenate(
        [head_shift[0], jnp.zeros((local_width,), jnp.float32), head_shift[1]]
    )
    mixed_low = (
        jnp.einsum("rd,dc->cr", normed_all, in_low, preferred_element_type=jnp.float32)
        + mixed_shift[:, None]
    ).astype(jnp.bfloat16)
    attended_low, log_totals = attend(mixed_low, spans)
    out_low = project_out.astype(jnp.bfloat16)
    attn_part = model_scatter(
        jnp.einsum(
            "cr,cd->rd", attended_low, out_low, preferred_element_type=jnp.float32
        ).astype(jnp.bfloat16),
        4,
    )
    middle = patch_values + attn_part + shift_rows[2]
    normed_two, norm_two_back = jax.vjp(layer_norm, middle, norm_gains[1], shift_rows[1])
    normed_low = normed_two.astype(jnp.bfloat16)
    out_grad = jnp.where(live_rows, cotangent, jnp.zeros_like(cotangent))
    out_grad_all = lax.all_gather(after(out_grad, normed_all), "mp", axis=0, tiled=True)
    normed_low, out_grad_all = lax.optimization_barrier((normed_low, out_grad_all))
    normed_two_all = model_gather(normed_low, 5)
    expand_low = expand_weight.astype(jnp.bfloat16)
    shrink_low = shrink_weight.astype(jnp.bfloat16)
    shift_part = lax.dynamic_slice_in_dim(expand_shift, model_index * local_hidden, local_hidden, 0)
    hidden_low, grad_before, two_share, ffn_share, shift_sum = mlp(
        normed_two_all, out_grad_all, expand_low, shrink_low, shift_part
    )
    grad_shrink = jnp.einsum(
        "rf,rd->fd", hidden_low, out_grad_all, preferred_element_type=jnp.float32
    ).astype(jnp.bfloat16)
    grad_expand = jnp.einsum(
        "rd,rf->df", normed_two_all, grad_before, preferred_element_type=jnp.float32
    ).astype(jnp.bfloat16)
    summed_expand, summed_shrink = lax.psum((grad_expand, grad_shrink), "dp")
    summed_expand = summed_expand.astype(jnp.float32)
    summed_shrink = summed_shrink.astype(jnp.float32)
    grad_expand_shift = lax.dynamic_update_slice_in_dim(
        jnp.zeros((FF,), jnp.float32), shift_sum[0], model_index * local_hidden, 0
    )
    grad_normed_two = model_scatter(two_share, 6)
    grad_middle_norm, gain_two_grad, shift_two_grad = norm_two_back(grad_normed_two)
    out_grad_values = out_grad.astype(jnp.float32)
    grad_middle = out_grad_values + grad_middle_norm
    middle_all = model_gather(grad_middle.astype(jnp.bfloat16), 7)
    grad_out = jnp.einsum("cr,rd->cd", attended_low, middle_all, preferred_element_type=jnp.float32)
    grad_attended = jnp.einsum(
        "cd,rd->cr", out_low, middle_all, preferred_element_type=jnp.float32
    ).astype(jnp.bfloat16)
    grad_mixed, head_sums = attend_back(mixed_low, attended_low, grad_attended, log_totals, spans)
    grad_in = jnp.einsum("rd,cr->dc", normed_all, grad_mixed, preferred_element_type=jnp.float32)
    grad_head = jnp.stack([head_sums[:local_width, 0], head_sums[local_width:, 0]])
    one_share = jnp.einsum(
        "cr,dc->rd", grad_mixed, in_low, preferred_element_type=jnp.float32
    ).astype(jnp.bfloat16)
    ffn_share = after(ffn_share, one_share)
    summed_out, summed_in = sum_groups(
        (grad_out.astype(jnp.bfloat16), grad_in.astype(jnp.bfloat16)), 8
    )
    summed_in = summed_in.astype(jnp.float32)
    summed_out = summed_out.astype(jnp.float32)
    grad_normed_one = lax.psum_scatter(
        one_share, "mp", scatter_dimension=0, tiled=True
    ).astype(jnp.float32)
    grad_patch_norm, gain_one_grad, shift_one_grad = norm_one_back(grad_normed_one)
    patch_grad = (grad_middle + grad_patch_norm).astype(jnp.bfloat16)
    gain_grads = jnp.stack([gain_one_grad, gain_two_grad])
    shift_grads = jnp.stack(
        [
            shift_one_grad,
            shift_two_grad,
            jnp.sum(grad_middle, axis=0),
            jnp.sum(out_grad_values, axis=0),
        ]
    )
    next_moment_in = muon_decay * moment_in + summed_in.reshape(D, 3, local_width)
    next_moment_out = muon_decay * moment_out + summed_out
    next_moment_expand = muon_decay * moment_expand + summed_expand
    next_moment_shrink = muon_decay * moment_shrink + summed_shrink
    matrices = [
        next_moment_in.reshape(D, 3 * local_width),
        next_moment_out,
        next_moment_expand,
        next_moment_shrink,
    ]
    orient = [True, False, True, False]
    lows = [matrix.astype(jnp.bfloat16) for matrix in matrices]
    own_gram = gram_exchange(gram_strips(*lows))
    ffn_part = lax.psum_scatter(
        ffn_share, "mp", scatter_dimension=0, tiled=True
    ).astype(jnp.float32)
    block_value = middle + ffn_part + shift_rows[3]
    block_out = jnp.where(live_rows, block_value, 0.0).astype(jnp.bfloat16)
    vector = jnp.concatenate(
        [gain_grads.reshape(-1), shift_grads.reshape(-1), grad_expand_shift]
    ).reshape(-1, 128)
    factors, vector_total, head_total = factor_exchange(
        sweep_chain(own_gram), vector, grad_head.reshape(-1, 128)
    )
    vector_total = vector_total.reshape(-1)
    gain_total = vector_total[: 2 * D].reshape(2, D)
    shift_total = vector_total[2 * D : 6 * D].reshape(4, D)
    expand_shift_total = vector_total[6 * D :]
    summed_head = head_total.reshape(2, local_width)
    scaled = [
        jnp.dot(factors[index], lows[index], preferred_element_type=jnp.float32)
        if orient[index]
        else jnp.einsum("rc,dc->rd", lows[index], factors[index], preferred_element_type=jnp.float32)
        for index in range(4)
    ]
    next_in = project_in - 1.25 * scaled[0].reshape(D, 3, local_width)
    next_out = project_out - 2.0 * scaled[1]
    next_expand = expand_weight - 1.0 * scaled[2]
    next_shrink = shrink_weight - 0.5 * scaled[3]
    vector_rate = 0.2 / math.sqrt(ROWS_GRP * dp_count)
    next_moment_gains = plain_decay * moment_gains + gain_total
    next_moment_shifts = plain_decay * moment_shifts + shift_total
    next_moment_head = plain_decay * moment_head + summed_head
    next_moment_expand_shift = plain_decay * moment_expand_shift + expand_shift_total
    next_gains = norm_gains - vector_rate * next_moment_gains
    next_shifts = shift_rows - vector_rate * next_moment_shifts
    next_head_shift = head_shift - vector_rate * next_moment_head
    next_expand_shift = expand_shift - vector_rate * next_moment_expand_shift
    return (
        block_out,
        patch_grad,
        next_in,
        next_out,
        next_expand,
        next_shrink,
        next_in.astype(jnp.bfloat16),
        next_out.astype(jnp.bfloat16),
        next_expand.astype(jnp.bfloat16),
        next_shrink.astype(jnp.bfloat16),
        next_moment_in,
        next_moment_out,
        next_moment_expand,
        next_moment_shrink,
        next_gains,
        next_shifts,
        next_head_shift,
        next_expand_shift,
        next_moment_gains,
        next_moment_shifts,
        next_moment_head,
        next_moment_expand_shift,
    )


def solution(mesh):
    placed = (
        P(("dp", "mp"), None),
        P(("dp", "mp"), None),
        P(),
        P(),
        P(None, None, "mp"),
        P("mp", None),
        P(None, "mp"),
        P("mp", None),
        P(None, None, "mp"),
        P("mp", None),
        P(None, "mp"),
        P("mp", None),
        P(),
        P(),
        P(None, "mp"),
        P(),
        P(),
        P(),
        P(None, "mp"),
        P(),
    )
    return jax.shard_map(
        on_device,
        mesh=mesh,
        in_specs=placed,
        out_specs=(
            P(("dp", "mp"), None),
            P(("dp", "mp"), None),
            P(None, None, "mp"),
            P("mp", None),
            P(None, "mp"),
            P("mp", None),
            P(None, None, "mp"),
            P("mp", None),
            P(None, "mp"),
            P("mp", None),
            P(None, None, "mp"),
            P("mp", None),
            P(None, "mp"),
            P("mp", None),
            P(),
            P(),
            P(None, "mp"),
            P(),
            P(),
            P(),
            P(None, "mp"),
            P(),
        ),
        check_vma=False,
    )
```
